256 devices in a mesh: dom: 64 (over y, z, core), rep: 4 (over x).
Axes of the slice: x: 4, y: 4, z: 8, core: 2. Of those that a mesh axis runs over, the one named last changes fastest.
Arguments:
- embedding: float32 [32768, 400], P('dom'), may hold values from -1.5 to 1.5
- adagrad_sum: float32 [32768], P('dom'), may hold values from 0.01 to 1
- row_lists: int32 [4, 64, 64, 16], P('rep', 'dom'), may hold values from 0 to 511, as said below
- source_slots: int32 [4, 64, 2, 512], P('rep', 'dom'), may hold values from 0 to 1023, as said below
- target_slots: int32 [4, 64, 2, 512], P('rep', 'dom'), may hold values from 0 to 1023, as said below
- negative_ids: int32 [4, 64, 2, 2, 512], P('rep', 'dom'), may hold values from 0 to 511
Outputs:
- new_embedding: float32 [32768, 400], P('dom')
- new_adagrad_sum: float32 [32768], P('dom')
The draws below stay inside these ranges and needn't reach their ends.
Inputs may be any that keep to these rules, and one draw needn't show every extreme that they name: `row_lists`: for each worker and owner, a count of leading entries are distinct rows of that owner and the other entries are 0. For the worker with index w along dom, the owners (w + c) mod 64, c < 4, have all 16 entries live; every other owner has 1 to 8 live entries. `source_slots`: every slot named is among the leading live entries of the worker's row list for its owner; entries k >= 8 are named only for the owners (w + c) mod 64, c < 4, of the worker with index w along dom. `target_slots`: every slot named is among the leading live entries of the worker's row list for its owner; entries k >= 8 are named only for the owners (w + c) mod 64, c < 4, of the worker with index w along dom.
All inputs are finite; a program needn't handle non-finite values.
Results may differ from the reference program's by a relative error of at most 0.0003.
Values sent between devices are 32-bit elements; how exact they have to be, the bound alone decides.
No kernel may reach another device: no remote copies, remote signals or barrier semaphores. Data moves between devices by JAX's collectives and lax.ppermute only.
A program may use at most 64 MiB of HBM per device.

```python
import math
import jax
import jax.numpy as jnp
from jax import lax

D = 400
ROWS_DEV = 512
EDGES = 512
NEGS = 512
BATCHES = 2
SLOTS = 16
HEAVY = 4
OWNERS = 64
GROUPS = 4
NODES = 32768


def plan_counts(key):
    base_key = jax.random.fold_in(key, 11)
    lowest = max(SLOTS // 4, 1)
    others = jax.random.randint(jax.random.fold_in(base_key, 3), (GROUPS, OWNERS, OWNERS), lowest, SLOTS // 2 + 1)
    workers = jnp.arange(OWNERS, dtype=jnp.int32)[:, None]
    owners = jnp.arange(OWNERS, dtype=jnp.int32)[None, :]
    heavy = (owners - workers) % OWNERS < HEAVY
    return jnp.where(heavy[None], SLOTS, others).astype(jnp.int32)


def edge_slots(key, which):
    counts = plan_counts(key)
    edge_key = jax.random.fold_in(key, 20 + which)
    shape = (GROUPS, OWNERS, BATCHES * EDGES)
    picks = jax.random.randint(jax.random.fold_in(edge_key, 1), shape, 0, OWNERS * SLOTS)
    owner = picks // SLOTS
    within = picks % SLOTS
    live = jnp.take_along_axis(counts, owner, axis=2)
    spread = owner * SLOTS + within % live
    workers = jnp.arange(OWNERS, dtype=jnp.int32)[None, :, None]
    reach = jax.random.randint(jax.random.fold_in(edge_key, 2), shape, 0, HEAVY)
    place = jax.random.randint(jax.random.fold_in(edge_key, 3), shape, 0, SLOTS)
    focused = (workers + reach) % OWNERS * SLOTS + place
    coin = jax.random.randint(jax.random.fold_in(edge_key, 4), shape, 0, 2)
    slots = jnp.where(coin == 0, focused, spread)
    return slots.reshape(GROUPS, OWNERS, BATCHES, EDGES).astype(jnp.int32)


def draw_row_lists(key, part):
    counts = plan_counts(key)
    list_key = jax.random.fold_in(key, 12)
    starts = jax.random.randint(jax.random.fold_in(list_key, 1), (GROUPS, OWNERS, OWNERS, 1), 0, ROWS_DEV)
    strides = 2 * jax.random.randint(jax.random.fold_in(list_key, 2), (GROUPS, OWNERS, OWNERS, 1), 0, ROWS_DEV // 2) + 1
    places = jnp.arange(SLOTS, dtype=jnp.int32)
    rows = (starts + places * strides) % ROWS_DEV
    return jnp.where(places < counts[..., None], rows, 0).astype(jnp.int32)


def draw_source_slots(key, part):
    return edge_slots(key, 0)


def draw_target_slots(key, part):
    return edge_slots(key, 1)


def with_ends(drawn, key, least, top_value):
    dims = drawn.shape
    spot = [jax.random.randint(jax.random.fold_in(key, axis), (), 0, dims[axis]) for axis in range(len(dims))]
    drawn = drawn.at[tuple(spot)].set(least)
    longest = dims.index(max(dims))
    spot[longest] = (spot[longest] + 1) % dims[longest]
    return drawn.at[tuple(spot)].set(top_value)


def shard_levels(stream_key, dims, shards, smallest, top_value):
    level = 1.0
    for axis_at, blocks in shards:
        steps = jax.random.uniform(jax.random.fold_in(jax.random.fold_in(stream_key, 6), axis_at), (blocks,), jnp.float32, smallest / len(shards), top_value / len(shards))
        level = level * jnp.repeat(jnp.exp(steps), dims[axis_at] // blocks).reshape((-1,) + (1,) * (len(dims) - 1 - axis_at))
    return level


def scatter_about(own_key, shape, width, most, shards=(), kind=jnp.bfloat16):
    factor_of = shard_levels(own_key, shape, shards, -0.22, 0.18) if shards else 1.0
    array = jax.random.normal(own_key, shape, jnp.float32) * width * factor_of
    return jnp.minimum(jnp.maximum(array, -most), most).astype(kind)


def setup_inputs(seed: int = 0) -> dict:
    streams_of = jax.random.split(jax.random.key(seed), 7)
    return {
        "embedding": scatter_about(streams_of[0], (NODES, D), 0.25, 1.5, ((0, 64),), jnp.float32),
        "adagrad_sum": jnp.clip(jnp.exp(math.log(1.0) - 4.6051702 * jax.random.uniform(streams_of[1], (NODES,), jnp.float32) ** shard_levels(streams_of[1], (NODES,), ((0, 64),), -0.2, 0.2)), 0.01, 1.0),
        "row_lists": draw_row_lists(jax.random.fold_in(streams_of[6], 71), 0),
        "source_slots": draw_source_slots(jax.random.fold_in(streams_of[6], 71), 0),
        "target_slots": draw_target_slots(jax.random.fold_in(streams_of[6], 71), 0),
        "negative_ids": with_ends(jax.random.randint(streams_of[5], (GROUPS, OWNERS, BATCHES, 2, NEGS), 0, EDGES), jax.random.fold_in(streams_of[5], 1), 0, EDGES - 1).astype(jnp.int32),
    }


learn_rate = 0.1

def batch_grads(buffer, sources, targets, neg_dst, neg_src):
    highest = lax.Precision.HIGHEST
    src_rows = buffer[sources]
    dst_rows = buffer[targets]
    neg_dst_rows = buffer[targets[neg_dst]]
    neg_src_rows = buffer[sources[neg_src]]
    samples = neg_dst.shape[0]
    positive = lax.optimization_barrier(jnp.sum(src_rows * dst_rows, axis=1))
    pos_weight = -jax.nn.sigmoid(-positive)[:, None]
    dst_scores = jnp.dot(src_rows, neg_dst_rows.T, precision=highest)
    src_scores = jnp.dot(dst_rows, neg_src_rows.T, precision=highest)
    dst_weight = jax.nn.sigmoid(dst_scores) / samples
    src_weight = jax.nn.sigmoid(src_scores) / samples
    grad_src = pos_weight * dst_rows + jnp.dot(dst_weight, neg_dst_rows, precision=highest)
    grad_dst = pos_weight * src_rows + jnp.dot(src_weight, neg_src_rows, precision=highest)
    grad_negd = jnp.dot(dst_weight.T, src_rows, precision=highest)
    grad_negs = jnp.dot(src_weight.T, dst_rows, precision=highest)
    gradient = jnp.zeros(buffer.shape, buffer.dtype)
    gradient = gradient.at[sources].add(grad_src).at[targets].add(grad_dst)
    gradient = gradient.at[targets[neg_dst]].add(grad_negd).at[sources[neg_src]].add(grad_negs)
    return gradient

def reference(embedding, adagrad_sum, row_lists, source_slots, target_slots, negative_ids):
    offsets = (jnp.arange(OWNERS, dtype=jnp.int32) * ROWS_DEV)[:, None]
    lists = row_lists.reshape(GROUPS * OWNERS, OWNERS, SLOTS)
    sources_all = source_slots.reshape(GROUPS * OWNERS, BATCHES, EDGES)
    targets_all = target_slots.reshape(GROUPS * OWNERS, BATCHES, EDGES)
    negatives = negative_ids.reshape(GROUPS * OWNERS, BATCHES, 2, NEGS)

    def worker(summed, inputs):
        request, sources, targets, negs = inputs
        global_rows = (request.astype(jnp.int32) + offsets).reshape(-1)
        buffer = embedding[global_rows]
        gradient = jnp.zeros(buffer.shape, buffer.dtype)
        for batch in range(BATCHES):
            gradient = gradient + batch_grads(buffer, sources[batch], targets[batch], negs[batch, 0], negs[batch, 1])
        return (summed.at[global_rows].add(gradient), None)
    row_grad, unused = lax.scan(worker, jnp.zeros(embedding.shape, embedding.dtype), (lists, sources_all, targets_all, negatives))
    new_sum = adagrad_sum + lax.optimization_barrier(jnp.mean(row_grad * row_grad, axis=1))
    new_rows = embedding - learn_rate * row_grad / jnp.sqrt(new_sum)[:, None]
    return (new_rows, new_sum)
```

```python
import jax
import jax.numpy as jnp
from jax import lax
from jax.experimental import pallas as pl
from jax.experimental.pallas import tpu as pltpu
from jax.sharding import PartitionSpec as P

HEAVY = 4
LEARN_RATE = 0.1
LANES = 128
WIDTHS = (104, 104, 96, 96)
STARTS = (0, 104, 208, 304)
f32 = jnp.float32
bf16 = jnp.bfloat16


def passed_along(value, axis, steps):
    count = lax.axis_size(axis)
    pairs = [(source, (source + steps) % count) for source in range(count)]
    return lax.ppermute(value, axis, pairs)


def exchanged(value, axis):
    return lax.all_to_all(value, axis, 0, 0, tiled=True)


def halves(x):
    high = x.astype(bf16)
    low = (x - high.astype(f32)).astype(bf16)
    return high, low


def mm(a, b):
    return jnp.dot(a, b, preferred_element_type=f32)


def mm_nt(a, b):
    return lax.dot_general(a, b, (((1,), (1,)), ((), ())), preferred_element_type=f32)


def serve_body(head_ids, tail_ids, rows, heads, tails):
    def eight(w, carry):
        for k in range(8):
            heads[pl.ds(w * 8 + k, 1), :] = rows[pl.ds(head_ids[w * 8 + k], 1), :]
        return carry

    lax.fori_loop(0, heads.shape[0] // 8, eight, 0, unroll=2)
    for k in range(tails.shape[0]):
        tails[pl.ds(k, 1), :] = rows[pl.ds(tail_ids[k], 1), :]


def serve(head_ids, tail_ids, rows):
    width = rows.shape[1]
    return pl.pallas_call(
        serve_body,
        grid_spec=pltpu.PrefetchScalarGridSpec(
            num_scalar_prefetch=2,
            grid=(1,),
            in_specs=[pl.BlockSpec(rows.shape, lambda i, a, b: (0, 0))],
            out_specs=[
                pl.BlockSpec((head_ids.shape[0], width), lambda i, a, b: (0, 0)),
                pl.BlockSpec((tail_ids.shape[0], width), lambda i, a, b: (0, 0)),
            ],
        ),
        out_shape=[
            jax.ShapeDtypeStruct((head_ids.shape[0], width), f32),
            jax.ShapeDtypeStruct((tail_ids.shape[0], width), f32),
        ],
        name="serve",
    )(head_ids, tail_ids, rows)


def prep_body(slots, negs, by_edge, by_slot, count_row, count_col):
    edges = count_row.shape[2]
    parts = slots.shape[1] // edges
    live = by_slot.shape[0]
    padded = by_edge.shape[1]
    one, zero = jnp.ones((), f32), jnp.zeros((), f32)
    for p in range(parts):
        row = slots[:, p * edges : (p + 1) * edges]
        down = lax.broadcasted_iota(jnp.int32, (live, edges), 0)
        by_slot[:, p * edges : (p + 1) * edges] = jnp.where(down == row, one, zero).astype(bf16)
        column = jnp.broadcast_to(row, (LANES, edges)).T
        across = lax.broadcasted_iota(jnp.int32, (edges, LANES), 1)
        for c in range(padded // LANES):
            by_edge[p * edges : (p + 1) * edges, c * LANES : (c + 1) * LANES] = jnp.where(
                across + c * LANES == column, one, zero
            ).astype(bf16)
        neg = negs[:, p * edges : (p + 1) * edges]
        down = lax.broadcasted_iota(jnp.int32, (edges, edges), 0)
        drawn = jnp.where(down == neg, one, zero).astype(bf16)
        if p % 2 == 0:
            count_row[p // 2] = mm_nt(jnp.ones((8, edges), bf16), drawn)
        else:
            count_col[p // 2] = mm(drawn, jnp.ones((edges, LANES), bf16))


def prep(slots, negs, edges, live, padded):
    total = slots.shape[1]
    batches = total // edges // 2
    return pl.pallas_call(
        prep_body,
        out_shape=[
            jax.ShapeDtypeStruct((total, padded), bf16),
            jax.ShapeDtypeStruct((live, total), bf16),
            jax.ShapeDtypeStruct((batches, 8, edges), f32),
            jax.ShapeDtypeStruct((batches, edges, LANES), f32),
        ],
        name="prep",
    )(slots, negs)


def grads_body(heads, tails, by_edge, by_slot, count_row, count_col, out_heads, out_tails, high, low, d_high, d_low):
    head_count = heads.shape[0]
    live = head_count + tails.shape[0]
    padded = by_edge.shape[1]
    width = heads.shape[1]
    batches, _, edges = count_row.shape
    high[:head_count, :], low[:head_count, :] = halves(heads[...])
    high[head_count:live, :], low[head_count:live, :] = halves(tails[...])
    high[live:, :] = jnp.zeros((padded - live, width), bf16)
    low[live:, :] = jnp.zeros((padded - live, width), bf16)
    for b in range(batches):
        picks = []
        for side in range(2):
            at = (2 * b + side) * edges
            chosen = by_edge[at : at + edges, :]
            picks.append((mm(chosen, high[...]).astype(bf16), mm(chosen, low[...]).astype(bf16)))
        (s_high, s_low), (t_high, t_low) = picks
        scores = mm_nt(s_high, t_high) + mm_nt(s_high, t_low) + mm_nt(s_low, t_high)
        decay = jnp.exp(-jnp.abs(scores))
        upper = 1.0 / (1.0 + decay)
        lower = decay * upper
        sure = scores >= 0
        weight = jnp.where(sure, upper, lower)
        missing = jnp.where(sure, lower, upper)
        counts = count_row[b, 0:1, :] + jnp.concatenate([count_col[b]] * (edges // LANES), axis=1)
        down = lax.broadcasted_iota(jnp.int32, (edges, edges), 0)
        across = lax.broadcasted_iota(jnp.int32, (edges, edges), 1)
        gain = weight * counts * (1.0 / edges) - jnp.where(down == across, missing, 0.0)
        g_high, g_low = halves(gain)
        d_s = mm(g_high, t_high) + mm(g_high, t_low) + mm(g_low, t_high)
        at = 2 * b * edges
        d_high[at : at + edges, :], d_low[at : at + edges, :] = halves(d_s)
        g_high, g_low = halves(gain.T)
        d_t = mm(g_high, s_high) + mm(g_high, s_low) + mm(g_low, s_high)
        at += edges
        d_high[at : at + edges, :], d_low[at : at + edges, :] = halves(d_t)
    summed = mm(by_slot[...], d_high[...]) + mm(by_slot[...], d_low[...])
    for q in range(width // LANES):
        out_heads[q] = summed[:head_count, q * LANES : (q + 1) * LANES]
    out_tails[...] = summed[head_count:, :]


def grads(heads, tails, by_edge, by_slot, count_row, count_col):
    head_count, width = heads.shape
    padded = by_edge.shape[1]
    total = by_edge.shape[0]
    return pl.pallas_call(
        grads_body,
        out_shape=[
            jax.ShapeDtypeStruct((width // LANES, head_count, LANES), f32),
            jax.ShapeDtypeStruct(tails.shape, f32),
        ],
        scratch_shapes=[
            pltpu.VMEM((padded, width), bf16),
            pltpu.VMEM((padded, width), bf16),
            pltpu.VMEM((total, width), bf16),
            pltpu.VMEM((total, width), bf16),
        ],
        name="grads",
    )(heads, tails, by_edge, by_slot, count_row, count_col)


def owner_body(back, tails, head_ids, tail_ids, out):
    rows = out.shape[1]

    def part(values, ids):
        down = lax.broadcasted_iota(jnp.int32, (rows, ids.shape[1]), 0)
        hot = jnp.where(down == ids, 1.0, 0.0).astype(bf16)
        high, low = halves(values)
        return mm(hot, high) + mm(hot, low)

    summed = part(back[...], head_ids[...]) + part(tails[...], tail_ids[...])
    out[...] = summed.T[: out.shape[0], :]


def owner(back, tails, head_ids, tail_ids, rows):
    return pl.pallas_call(
        owner_body,
        out_shape=jax.ShapeDtypeStruct((max(WIDTHS), rows), f32),
        name="owner",
    )(back, tails, head_ids, tail_ids)


def update_body(quarters, rows, sums, new_rows, new_sums):
    squares = jnp.zeros(sums.shape, f32)
    for q in range(quarters.shape[0]):
        squares += jnp.sum(quarters[q] * quarters[q], axis=0, keepdims=True)
    fresh = sums[...] + squares * (1.0 / rows.shape[1])
    new_sums[...] = fresh
    scale = LEARN_RATE / jnp.sqrt(fresh)
    step = jnp.concatenate([quarters[q, :w, :] * scale for q, w in enumerate(WIDTHS)], axis=0)
    new_rows[...] = rows[...] - step.T


def update(quarters, rows, sums):
    return pl.pallas_call(
        update_body,
        out_shape=[
            jax.ShapeDtypeStruct(rows.shape, f32),
            jax.ShapeDtypeStruct(sums.shape, f32),
        ],
        name="update",
    )(quarters, rows, sums)


def compact(slots, here, owners, capacity):
    half = capacity // 2
    who, k = slots // capacity, slots % capacity
    return jnp.where(k < half, who * half + k, owners * half + (who - here) % owners * half + k - half)


def local(embedding, adagrad_sum, row_lists, source_slots, target_slots, negative_ids):
    requests = row_lists[0, 0]
    owners, capacity = requests.shape
    half = capacity // 2
    rows = embedding.shape[0]
    groups = lax.axis_size("rep")
    edges = source_slots.shape[3]
    here = lax.axis_index("dom")
    incoming = exchanged(requests, "dom")
    spread = jnp.concatenate(
        [jnp.pad(embedding[:, s : s + w], ((0, 0), (0, LANES - w))) for s, w in zip(STARTS, WIDTHS)],
        axis=1,
    )
    slots = jnp.stack([source_slots[0, 0], target_slots[0, 0]], axis=1).reshape(1, -1)
    slots = compact(slots, here, owners, capacity)
    live = owners * half + HEAVY * half
    padded = -(-live // LANES) * LANES
    plan = prep(slots, negative_ids[0, 0].reshape(1, -1), edges, live, padded)

    askers = (here - jnp.arange(HEAVY)) % owners
    tail_ids = incoming[askers, half:].reshape(-1)
    head_ids = incoming[:, :half].reshape(-1)
    heads, tails = serve(head_ids, tail_ids, spread)
    tails = tails.reshape(HEAVY, half, -1)
    tails = jnp.concatenate(
        [tails[0]] + [passed_along(tails[r], "dom", -r) for r in range(1, HEAVY)], axis=0
    )
    heads = exchanged(heads.reshape(owners, half, -1), "dom").reshape(owners * half, -1)
    all_ids = exchanged(
        jnp.broadcast_to(jnp.concatenate([head_ids, tail_ids])[None], (groups, live)), "rep"
    )

    head_grads, tail_grads = grads(heads, tails, *plan)
    tail_grads = tail_grads.reshape(HEAVY, half, -1)
    tail_grads = jnp.concatenate(
        [tail_grads[0]] + [passed_along(tail_grads[r], "dom", r) for r in range(1, HEAVY)], axis=0
    )
    tail_grads = jnp.moveaxis(tail_grads.reshape(HEAVY * half, groups, LANES), 1, 0)
    tail_back = exchanged(tail_grads, "rep").reshape(-1, LANES)
    back = exchanged(head_grads.reshape(groups * owners, half, LANES), ("rep", "dom"))
    quarter = owner(
        back.reshape(-1, LANES),
        tail_back,
        all_ids[:, : owners * half].reshape(1, -1),
        all_ids[:, owners * half :].reshape(1, -1),
        rows,
    )
    quarters = exchanged(jnp.broadcast_to(quarter[None], (groups, *quarter.shape)), "rep")
    new_rows, new_sums = update(quarters, embedding, adagrad_sum.reshape(1, -1))
    return new_rows, new_sums.reshape(-1)


def solution(mesh):
    in_specs = (
        P("dom", None),
        P("dom"),
        P("rep", "dom", None, None),
        P("rep", "dom", None, None),
        P("rep", "dom", None, None),
        P("rep", "dom", None, None, None),
    )
    out_specs = (P("dom", None), P("dom"))
    return jax.shard_map(local, mesh=mesh, in_specs=in_specs, out_specs=out_specs, check_vma=False)
```

```python
import jax
import jax.numpy as jnp
from jax import lax
from jax.experimental import pallas as pl
from jax.experimental.pallas import tpu as pltpu
from jax.sharding import PartitionSpec as P


HEAVY = 4
LEARN_RATE = 0.1
LANES = 128
WIDTHS = (104, 104, 96, 96)
STARTS = (0, 104, 208, 304)
f32 = jnp.float32
bf16 = jnp.bfloat16


def passed_along(value, axis, steps):
    count = lax.axis_size(axis)
    pairs = [(source, (source + steps) % count) for source in range(count)]
    return lax.ppermute(value, axis, pairs)


def exchanged(value, axis):
    return lax.all_to_all(value, axis, 0, 0, tiled=True)


def halves(x):
    high = x.astype(bf16)
    low = (x - high.astype(f32)).astype(bf16)
    return high, low


def mm(a, b):
    return jnp.dot(a, b, preferred_element_type=f32)


def mm_nt(a, b):
    return lax.dot_general(a, b, (((1,), (1,)), ((), ())), preferred_element_type=f32)


def spread_body(columns, out):
    rows = columns.shape[1]
    for q, (start, w) in enumerate(zip(STARTS, WIDTHS)):
        piece = columns[start : start + w, :]
        if w < LANES:
            piece = jnp.concatenate([piece, jnp.zeros((LANES - w, rows), f32)], axis=0)
        out[:, q * LANES : (q + 1) * LANES] = piece.T


def spread_rows(columns):
    return pl.pallas_call(
        spread_body,
        out_shape=jax.ShapeDtypeStruct((columns.shape[1], LANES * len(WIDTHS)), f32),
        name="spread",
    )(columns)


def serve_body(ids, here, rows, heads, tails):
    owners = ids.shape[0] // 16

    def eight(w, carry):
        for k in range(8):
            heads[pl.ds(w * 8 + k, 1), :] = rows[pl.ds(ids[w * 16 + k], 1), :]
        return carry

    lax.fori_loop(0, owners, eight, 0, unroll=4)
    for reach in range(HEAVY):
        asker = (here[0] + owners - reach) % owners
        for k in range(8):
            tails[reach * 8 + k : reach * 8 + k + 1, :] = rows[pl.ds(ids[asker * 16 + 8 + k], 1), :]


def serve(ids, here, rows):
    width = rows.shape[1]
    head_count = ids.shape[0] // 2
    return pl.pallas_call(
        serve_body,
        grid_spec=pltpu.PrefetchScalarGridSpec(
            num_scalar_prefetch=2,
            grid=(1,),
            in_specs=[pl.BlockSpec(rows.shape, lambda i, a, b: (0, 0))],
            out_specs=[
                pl.BlockSpec((head_count, width), lambda i, a, b: (0, 0)),
                pl.BlockSpec((HEAVY * 8, width), lambda i, a, b: (0, 0)),
            ],
        ),
        out_shape=[
            jax.ShapeDtypeStruct((head_count, width), f32),
            jax.ShapeDtypeStruct((HEAVY * 8, width), f32),
        ],
        name="serve",
    )(ids, here, rows)


def prep_body(slots, negs, by_edge, by_slot, count_row, count_col):
    edges = count_row.shape[2]
    parts = slots.shape[1] // edges
    live = by_slot.shape[0]
    padded = by_edge.shape[1]
    one, zero = jnp.ones((), f32), jnp.zeros((), f32)
    for p in range(parts):
        row = slots[:, p * edges : (p + 1) * edges]
        down = lax.broadcasted_iota(jnp.int32, (live, edges), 0)
        by_slot[:, p * edges : (p + 1) * edges] = jnp.where(down == row, one, zero).astype(bf16)
        column = jnp.broadcast_to(row, (LANES, edges)).T
        across = lax.broadcasted_iota(jnp.int32, (edges, LANES), 1)
        for c in range(padded // LANES):
            by_edge[p * edges : (p + 1) * edges, c * LANES : (c + 1) * LANES] = jnp.where(
                across + c * LANES == column, one, zero
            ).astype(bf16)
        neg = negs[:, p * edges : (p + 1) * edges]
        down = lax.broadcasted_iota(jnp.int32, (edges, edges), 0)
        drawn = jnp.where(down == neg, one, zero).astype(bf16)
        if p % 2 == 0:
            count_row[p // 2] = mm_nt(jnp.ones((8, edges), bf16), drawn)
        else:
            count_col[p // 2] = mm(drawn, jnp.ones((edges, LANES), bf16))


def prep(slots, negs, edges, live, padded):
    total = slots.shape[1]
    batches = total // edges // 2
    return pl.pallas_call(
        prep_body,
        out_shape=[
            jax.ShapeDtypeStruct((total, padded), bf16),
            jax.ShapeDtypeStruct((live, total), bf16),
            jax.ShapeDtypeStruct((batches, 8, edges), f32),
            jax.ShapeDtypeStruct((batches, edges, LANES), f32),
        ],
        name="prep",
    )(slots, negs)


def grads_body(heads, tails, by_edge, by_slot, count_row, count_col, ahead, out_heads, out_tails, high, low, d_high, d_low):
    head_count = heads.shape[0]
    live = head_count + tails.shape[0]
    padded = by_edge.shape[1]
    width = heads.shape[1]
    batches, _, edges = count_row.shape
    high[:head_count, :], low[:head_count, :] = halves(heads[...])
    high[head_count:live, :], low[head_count:live, :] = halves(tails[...])
    high[live:, :] = jnp.zeros((padded - live, width), bf16)
    low[live:, :] = jnp.zeros((padded - live, width), bf16)
    for b in range(batches):
        picks = []
        for side in range(2):
            at = (2 * b + side) * edges
            chosen = by_edge[at : at + edges, :]
            picks.append((mm(chosen, high[...]).astype(bf16), mm(chosen, low[...]).astype(bf16)))
        (s_high, s_low), (t_high, t_low) = picks
        scores = mm_nt(s_high, t_high) + mm_nt(s_high, t_low) + mm_nt(s_low, t_high)
        decay = jnp.exp(-jnp.abs(scores))
        upper = 1.0 / (1.0 + decay)
        lower = decay * upper
        sure = scores >= 0
        weight = jnp.where(sure, upper, lower)
        missing = jnp.where(sure, lower, upper)
        counts = count_row[b, 0:1, :] + jnp.concatenate([count_col[b]] * (edges // LANES), axis=1)
        down = lax.broadcasted_iota(jnp.int32, (edges, edges), 0)
        across = lax.broadcasted_iota(jnp.int32, (edges, edges), 1)
        gain = weight * counts * (1.0 / edges) - jnp.where(down == across, missing, 0.0)
        g_high, g_low = halves(gain)
        d_s = mm(g_high, t_high) + mm(g_high, t_low) + mm(g_low, t_high)
        at = 2 * b * edges
        d_high[at : at + edges, :], d_low[at : at + edges, :] = halves(d_s)
        g_high, g_low = halves(gain.T)
        d_t = mm(g_high, s_high) + mm(g_high, s_low) + mm(g_low, s_high)
        at += edges
        d_high[at : at + edges, :], d_low[at : at + edges, :] = halves(d_t)
    summed = mm(by_slot[...], d_high[...]) + mm(by_slot[...], d_low[...])
    for q in range(width // LANES):
        out_heads[q] = summed[:head_count, q * LANES : (q + 1) * LANES]
    out_tails[...] = summed[head_count:, :]


def grads(heads, tails, by_edge, by_slot, count_row, count_col, ahead):
    head_count, width = heads.shape
    padded = by_edge.shape[1]
    total = by_edge.shape[0]
    vmem = pl.BlockSpec(memory_space=pltpu.VMEM)
    return pl.pallas_call(
        grads_body,
        in_specs=[vmem] * 6 + [pl.BlockSpec(memory_space=pl.ANY)],
        out_shape=[
            jax.ShapeDtypeStruct((width // LANES, head_count, LANES), f32),
            jax.ShapeDtypeStruct(tails.shape, f32),
        ],
        scratch_shapes=[
            pltpu.VMEM((padded, width), bf16),
            pltpu.VMEM((padded, width), bf16),
            pltpu.VMEM((total, width), bf16),
            pltpu.VMEM((total, width), bf16),
        ],
        name="grads",
    )(heads, tails, by_edge, by_slot, count_row, count_col, ahead)


def hot_body(me, *refs):
    lists, hot = refs[:-1], refs[-1]
    rows = hot.shape[0]
    groups = len(lists)
    tail_count = HEAVY * 8
    head_count = lists[0].shape[1] - tail_count
    for s, ids in enumerate(lists):
        group = (me[0] + s) % groups
        down = lax.broadcasted_iota(jnp.int32, (rows, head_count), 0)
        spot = pl.multiple_of(group * head_count, LANES)
        hot[:, pl.ds(spot, head_count)] = jnp.where(down == ids[:, :head_count], 1.0, 0.0).astype(bf16)
    tails = jnp.concatenate([ids[:, head_count:] for ids in lists], axis=1)
    down = lax.broadcasted_iota(jnp.int32, (rows, tails.shape[1]), 0)
    hot[:, groups * head_count :] = jnp.where(down == tails, 1.0, 0.0).astype(bf16)


def hot_rows(me, lists, rows):
    vmem = pl.BlockSpec(memory_space=pltpu.VMEM)
    return pl.pallas_call(
        hot_body,
        in_specs=[pl.BlockSpec(memory_space=pltpu.SMEM)] + [vmem] * len(lists),
        out_shape=jax.ShapeDtypeStruct((rows, len(lists) * lists[0].shape[1]), bf16),
        name="hot",
    )(me, *lists)


def owner_body(back, tails, hot, out):
    count = back.shape[0]
    high, low = halves(back[...])
    summed = mm(hot[:, :count], high) + mm(hot[:, :count], low)
    high, low = halves(tails[...])
    summed += mm(hot[:, count:], high) + mm(hot[:, count:], low)
    out[...] = summed.T[: out.shape[0], :]


def owner(back, tails, hot):
    return pl.pallas_call(
        owner_body,
        out_shape=jax.ShapeDtypeStruct((max(WIDTHS), hot.shape[0]), f32),
        name="owner",
    )(back, tails, hot)


def update_body(me, own, next1, next2, next3, rows, sums, new_rows, new_sums, quarters, sems):
    copies = []
    for s, piece in enumerate((own, next1, next2, next3)):
        spot = (me[0] + 4 - s) % 4
        copies.append(pltpu.make_async_copy(piece, quarters.at[spot], sems.at[s]))
        copies[-1].start()
    for copy in copies:
        copy.wait()
    squares = jnp.zeros(sums.shape, f32)
    for q in range(len(WIDTHS)):
        squares += jnp.sum(quarters[q] * quarters[q], axis=0, keepdims=True)
    fresh = sums[...] + squares * (1.0 / rows.shape[0])
    new_sums[...] = fresh
    scale = LEARN_RATE / jnp.sqrt(fresh)
    for q, (start, w) in enumerate(zip(STARTS, WIDTHS)):
        new_rows[start : start + w, :] = rows[start : start + w, :] - quarters[q, :w, :] * scale


def update(me, pieces, rows, sums):
    vmem = pl.BlockSpec(memory_space=pltpu.VMEM)
    return pl.pallas_call(
        update_body,
        in_specs=[pl.BlockSpec(memory_space=pltpu.SMEM)]
        + [pl.BlockSpec(memory_space=pl.ANY)] * len(pieces)
        + [vmem, vmem],
        out_shape=[
            jax.ShapeDtypeStruct(rows.shape, f32),
            jax.ShapeDtypeStruct(sums.shape, f32),
        ],
        scratch_shapes=[
            pltpu.VMEM((len(pieces), *pieces[0].shape), f32),
            pltpu.SemaphoreType.DMA((len(pieces),)),
        ],
        name="update",
    )(me, *pieces, rows, sums)


def compact(slots, here, owners, capacity):
    half = capacity // 2
    who, k = slots // capacity, slots % capacity
    return jnp.where(k < half, who * half + k, owners * half + (who - here) % owners * half + k - half)


def local(embedding, adagrad_sum, row_lists, source_slots, target_slots, negative_ids):
    requests = row_lists[0, 0]
    owners, capacity = requests.shape
    half = capacity // 2
    rows = embedding.shape[0]
    groups = lax.axis_size("rep")
    edges = source_slots.shape[3]
    here = lax.axis_index("dom")
    incoming = exchanged(requests, "dom")
    columns = embedding.T
    spread = spread_rows(columns)
    slots = jnp.stack([source_slots[0, 0], target_slots[0, 0]], axis=1).reshape(1, -1)
    slots = compact(slots, here, owners, capacity)
    live = owners * half + HEAVY * half
    padded = -(-live // LANES) * LANES
    plan = prep(slots, negative_ids[0, 0].reshape(1, -1), edges, live, padded)

    heads, tails = serve(incoming.reshape(-1), here.reshape(1).astype(jnp.int32), spread)
    tails = tails.reshape(HEAVY, half, -1)
    tails = jnp.concatenate(
        [tails[0]] + [passed_along(tails[r], "dom", -r) for r in range(1, HEAVY)], axis=0
    )
    heads = exchanged(heads.reshape(owners, half, -1), "dom").reshape(owners * half, -1)
    me = lax.axis_index("rep")
    mine = me.reshape(1).astype(jnp.int32)
    askers = jnp.arange(owners)[None, :] == ((here - jnp.arange(HEAVY)) % owners)[:, None]
    tail_ids = jnp.sum(jnp.where(askers[:, :, None], incoming[None, :, half:], 0), axis=1)
    ids = jnp.concatenate([incoming[:, :half].reshape(1, -1), tail_ids.reshape(1, -1)], axis=1)
    near = [ids] + [passed_along(ids, "rep", -s) for s in range(1, groups)]
    hot = hot_rows(mine, near, rows)

    head_grads, tail_grads = grads(heads, tails, *plan, hot)
    tail_grads = tail_grads.reshape(HEAVY, half, -1)
    tail_grads = jnp.concatenate(
        [tail_grads[0]] + [passed_along(tail_grads[r], "dom", r) for r in range(1, HEAVY)], axis=0
    )
    tail_grads = jnp.moveaxis(tail_grads.reshape(HEAVY * half, groups, LANES), 1, 0)
    wanted = [
        lax.dynamic_index_in_dim(tail_grads, (me + groups - s) % groups, 0, keepdims=False)
        for s in range(groups)
    ]
    tail_back = jnp.concatenate(
        [wanted[0]] + [passed_along(wanted[s], "rep", -s) for s in range(1, groups)], axis=0
    )
    back = exchanged(head_grads.reshape(groups * owners, half, LANES), ("rep", "dom"))
    quarter = owner(back.reshape(-1, LANES), tail_back, hot)
    pieces = [quarter] + [passed_along(quarter, "rep", s) for s in range(1, len(WIDTHS))]
    new_rows, new_sums = update(mine, pieces, columns, adagrad_sum.reshape(1, -1))
    return new_rows.T, new_sums.reshape(-1)


def solution(mesh):
    in_specs = (
        P("dom", None),
        P("dom"),
        P("rep", "dom", None, None),
        P("rep", "dom", None, None),
        P("rep", "dom", None, None),
        P("rep", "dom", None, None, None),
    )
    out_specs = (P("dom", None), P("dom"))

    return jax.shard_map(local, mesh=mesh, in_specs=in_specs, out_specs=out_specs, check_vma=False)
```

```python
import jax
import jax.numpy as jnp
from jax import lax
from jax.experimental import pallas as pl
from jax.experimental.pallas import tpu as pltpu
from jax.sharding import PartitionSpec as P


HEAVY = 4
LEARN_RATE = 0.1
LANES = 128
WIDTHS = (104, 104, 96, 96)
STARTS = (0, 104, 208, 304)
f32 = jnp.float32
bf16 = jnp.bfloat16


def passed_along(value, axis, steps):
    count = lax.axis_size(axis)
    pairs = [(source, (source + steps) % count) for source in range(count)]
    return lax.ppermute(value, axis, pairs)


def exchanged(value, axis):
    return lax.all_to_all(value, axis, 0, 0, tiled=True)


def halves(x):
    high = x.astype(bf16)
    low = (x - high.astype(f32)).astype(bf16)
    return high, low


VMEM = pl.BlockSpec(memory_space=pltpu.VMEM)
SMEM = pl.BlockSpec(memory_space=pltpu.SMEM)
HBM = pl.BlockSpec(memory_space=pltpu.HBM)


def room(mib):
    return pltpu.CompilerParams(vmem_limit_bytes=mib << 20)


def far(x):
    return pltpu.with_memory_space_constraint(x, pltpu.HBM)


def near(x):
    return pltpu.with_memory_space_constraint(x, pltpu.VMEM)


def mm(a, b):
    return jnp.dot(a, b, preferred_element_type=f32)


def mm_nt(a, b):
    return lax.dot_general(a, b, (((1,), (1,)), ((), ())), preferred_element_type=f32)


def spread_body(columns, out):
    rows = columns.shape[1]
    for q, (start, w) in enumerate(zip(STARTS, WIDTHS)):
        piece = columns[start : start + w, :]
        if w < LANES:
            piece = jnp.concatenate([piece, jnp.zeros((LANES - w, rows), f32)], axis=0)
        out[:, q * LANES : (q + 1) * LANES] = piece.T


def spread_rows(columns):
    return pl.pallas_call(
        spread_body,
        out_specs=VMEM,
        out_shape=pltpu.VMEM((columns.shape[1], LANES * len(WIDTHS)), f32),
        compiler_params=room(16),
        name="spread",
    )(columns)


def serve_body(ids, here, rows, heads, tails, picked, sems):
    owners = ids.shape[0]
    parts = sems.shape[0]
    each = owners // parts

    def eight(w, carry):
        taken = [rows[pl.ds(ids[w, 0, k], 1), :] for k in range(8)]
        for k in range(8):
            picked[pl.ds(w * 8 + k, 1), :] = taken[k]
        return carry

    for reach in range(HEAVY):
        asker = (here[0] + owners - reach) % owners
        for k in range(8):
            tails[reach * 8 + k : reach * 8 + k + 1, :] = rows[pl.ds(ids[asker, 0, 8 + k], 1), :]
    copies = []
    for part in range(parts):
        lax.fori_loop(part * each, (part + 1) * each, eight, 0, unroll=4)
        span = pl.ds(part * each * 8, each * 8)
        copies.append(pltpu.make_async_copy(picked.at[span], heads.at[span], sems.at[part]))
        copies[-1].start()
    for copy in copies:
        copy.wait()


def serve(ids, here, rows):
    width = rows.shape[1]
    head_count = ids.shape[0] * 8
    return pl.pallas_call(
        serve_body,
        in_specs=[SMEM, SMEM, VMEM],
        out_specs=[HBM, VMEM],
        out_shape=[
            pltpu.HBM((head_count, width), f32),
            jax.ShapeDtypeStruct((HEAVY * 8, width), f32),
        ],
        scratch_shapes=[pltpu.VMEM((head_count, width), f32), pltpu.SemaphoreType.DMA((4,))],
        compiler_params=room(16),
        name="serve",
    )(ids, here, near(rows))


def prep_body(slots, negs, by_edge, by_slot, count_row, count_col):
    edges = count_row.shape[2]
    parts = slots.shape[1] // edges
    live = by_slot.shape[0]
    padded = by_edge.shape[1]
    one, zero = jnp.ones((), f32), jnp.zeros((), f32)
    for p in range(parts):
        row = slots[:, p * edges : (p + 1) * edges]
        down = lax.broadcasted_iota(jnp.int32, (live, edges), 0)
        by_slot[:, p * edges : (p + 1) * edges] = jnp.where(down == row, one, zero).astype(bf16)
        column = jnp.broadcast_to(row, (LANES, edges)).T
        across = lax.broadcasted_iota(jnp.int32, (edges, LANES), 1)
        for c in range(padded // LANES):
            by_edge[p * edges : (p + 1) * edges, c * LANES : (c + 1) * LANES] = jnp.where(
                across + c * LANES == column, one, zero
            ).astype(bf16)
        neg = negs[:, p * edges : (p + 1) * edges]
        down = lax.broadcasted_iota(jnp.int32, (edges, edges), 0)
        drawn = jnp.where(down == neg, one, zero).astype(bf16)
        if p % 2 == 0:
            count_row[p // 2] = mm_nt(jnp.ones((8, edges), bf16), drawn)
        else:
            count_col[p // 2] = mm(drawn, jnp.ones((edges, LANES), bf16))


def prep(slots, negs, edges, live, padded):
    total = slots.shape[1]
    batches = total // edges // 2
    return pl.pallas_call(
        prep_body,
        out_shape=[
            pltpu.HBM((total, padded), bf16),
            pltpu.HBM((live, total), bf16),
            pltpu.HBM((batches, 8, edges), f32),
            pltpu.HBM((batches, edges, LANES), f32),
        ],
        compiler_params=room(24),
        name="prep",
    )(slots, negs)


def grads_body(heads, tails, by_edge, by_slot, count_row, count_col, ahead, out_heads, out_tails,
               high, low, d_high, d_low, edge_part, slot_part, summed, in_sems, out_sems):
    head_count = heads.shape[0]
    live = head_count + tails.shape[0]
    padded = by_edge.shape[1]
    width = heads.shape[1]
    batches, _, edges = count_row.shape
    loads = []
    for p in range(2 * batches):
        span = pl.ds(p * edges, edges)
        loads.append(pltpu.make_async_copy(by_edge.at[span], edge_part.at[span], in_sems.at[p]))
        loads[-1].start()
    last = pltpu.make_async_copy(by_slot, slot_part, in_sems.at[2 * batches])
    last.start()
    high[:head_count, :], low[:head_count, :] = halves(heads[...])
    high[head_count:live, :], low[head_count:live, :] = halves(tails[...])
    high[live:, :] = jnp.zeros((padded - live, width), bf16)
    low[live:, :] = jnp.zeros((padded - live, width), bf16)
    for b in range(batches):
        picks = []
        for side in range(2):
            at = (2 * b + side) * edges
            loads[2 * b + side].wait()
            chosen = edge_part[at : at + edges, :]
            picks.append((mm(chosen, high[...]).astype(bf16), mm(chosen, low[...]).astype(bf16)))
        (s_high, s_low), (t_high, t_low) = picks
        scores = mm_nt(s_high, t_high) + mm_nt(s_high, t_low) + mm_nt(s_low, t_high)
        decay = jnp.exp(-jnp.abs(scores))
        upper = 1.0 / (1.0 + decay)
        lower = decay * upper
        sure = scores >= 0
        weight = jnp.where(sure, upper, lower)
        missing = jnp.where(sure, lower, upper)
        counts = count_row[b, 0:1, :] + jnp.concatenate([count_col[b]] * (edges // LANES), axis=1)
        down = lax.broadcasted_iota(jnp.int32, (edges, edges), 0)
        across = lax.broadcasted_iota(jnp.int32, (edges, edges), 1)
        gain = weight * counts * (1.0 / edges) - jnp.where(down == across, missing, 0.0)
        g_high, g_low = halves(gain)
        d_s = mm(g_high, t_high) + mm(g_high, t_low) + mm(g_low, t_high)
        at = 2 * b * edges
        d_high[at : at + edges, :], d_low[at : at + edges, :] = halves(d_s)
        g_high, g_low = halves(gain.T)
        d_t = mm(g_high, s_high) + mm(g_high, s_low) + mm(g_low, s_high)
        at += edges
        d_high[at : at + edges, :], d_low[at : at + edges, :] = halves(d_t)
    last.wait()
    stores = []
    block = 2 * LANES
    for h in range(width // block):
        span = slice(h * block, (h + 1) * block)
        part = mm(slot_part[...], d_high[:, span]) + mm(slot_part[...], d_low[:, span])
        for q in range(2):
            summed[2 * h + q] = part[:head_count, q * LANES : (q + 1) * LANES]
        out_tails[:, span] = part[head_count:, :]
        stores.append(
            pltpu.make_async_copy(summed.at[pl.ds(2 * h, 2)], out_heads.at[pl.ds(2 * h, 2)], out_sems.at[h])
        )
        stores[-1].start()
    for store in stores:
        store.wait()


def grads(heads, tails, by_edge, by_slot, count_row, count_col, ahead):
    head_count, width = heads.shape
    padded = by_edge.shape[1]
    total = by_edge.shape[0]
    shape = (width // LANES, head_count, LANES)
    return pl.pallas_call(
        grads_body,
        in_specs=[VMEM, VMEM, HBM, HBM, VMEM, VMEM, HBM],
        out_specs=[HBM, VMEM],
        out_shape=[pltpu.HBM(shape, f32), jax.ShapeDtypeStruct(tails.shape, f32)],
        scratch_shapes=[
            pltpu.VMEM((padded, width), bf16),
            pltpu.VMEM((padded, width), bf16),
            pltpu.VMEM((total, width), bf16),
            pltpu.VMEM((total, width), bf16),
            pltpu.VMEM(by_edge.shape, bf16),
            pltpu.VMEM(by_slot.shape, bf16),
            pltpu.VMEM(shape, f32),
            pltpu.SemaphoreType.DMA((2 * count_row.shape[0] + 1,)),
            pltpu.SemaphoreType.DMA((width // LANES // 2,)),
        ],
        compiler_params=room(48),
        name="grads",
    )(near(heads), tails, far(by_edge), far(by_slot), count_row, count_col, far(ahead))


def hot_body(me, *refs):
    lists, hot = refs[:-1], refs[-1]
    rows = hot.shape[0]
    groups = len(lists)
    tail_count = HEAVY * 8
    head_count = lists[0].shape[1] - tail_count
    for s, ids in enumerate(lists):
        group = (me[0] + s) % groups
        down = lax.broadcasted_iota(jnp.int32, (rows, head_count), 0)
        spot = pl.multiple_of(group * head_count, LANES)
        hot[:, pl.ds(spot, head_count)] = jnp.where(down == ids[:, :head_count], 1.0, 0.0).astype(bf16)
    tails = jnp.concatenate([ids[:, head_count:] for ids in lists], axis=1)
    down = lax.broadcasted_iota(jnp.int32, (rows, tails.shape[1]), 0)
    hot[:, groups * head_count :] = jnp.where(down == tails, 1.0, 0.0).astype(bf16)


def hot_rows(me, lists, rows):
    vmem = pl.BlockSpec(memory_space=pltpu.VMEM)
    return pl.pallas_call(
        hot_body,
        in_specs=[pl.BlockSpec(memory_space=pltpu.SMEM)] + [vmem] * len(lists),
        out_shape=pltpu.HBM((rows, len(lists) * lists[0].shape[1]), bf16),
        compiler_params=room(16),
        name="hot",
    )(me, *lists)


def owner_body(back, tails, hot, out, spots, sems):
    count = back.shape[0]
    parts = sems.shape[0] - 1
    each = count // parts
    spans = [(p * each, each) for p in range(parts)] + [(count, tails.shape[0])]
    loads = []
    for p, (at, size) in enumerate(spans):
        loads.append(pltpu.make_async_copy(hot.at[:, pl.ds(at, size)], spots.at[:, pl.ds(at, size)], sems.at[p]))
        loads[-1].start()
    summed = jnp.zeros((hot.shape[0], LANES), f32)
    for p, (at, size) in enumerate(spans):
        values = back[at : at + size, :] if p < parts else tails[...]
        both = jnp.concatenate(halves(values), axis=1)
        loads[p].wait()
        part = mm(spots[:, at : at + size], both)
        summed += part[:, :LANES] + part[:, LANES:]
    out[...] = summed.T[: out.shape[0], :]


def owner(back, tails, hot):
    return pl.pallas_call(
        owner_body,
        in_specs=[VMEM, VMEM, HBM],
        out_specs=VMEM,
        out_shape=jax.ShapeDtypeStruct((max(WIDTHS), hot.shape[0]), f32),
        scratch_shapes=[pltpu.VMEM(hot.shape, bf16), pltpu.SemaphoreType.DMA((5,))],
        compiler_params=room(16),
        name="owner",
    )(near(back), tails, far(hot))


def update_body(me, own, next1, next2, next3, rows, sums, new_rows, new_sums, quarters, fresh_rows, sems):
    for s, piece in enumerate((own, next1, next2, next3)):
        quarters[(me[0] + 4 - s) % 4] = piece[...]
    squares = jnp.zeros(sums.shape, f32)
    for q in range(len(WIDTHS)):
        squares += jnp.sum(quarters[q] * quarters[q], axis=0, keepdims=True)
    fresh = sums[...] + squares * (1.0 / rows.shape[0])
    new_sums[...] = fresh
    scale = LEARN_RATE / jnp.sqrt(fresh)
    stores = []
    for q, (start, w) in enumerate(zip(STARTS, WIDTHS)):
        fresh_rows[start : start + w, :] = rows[start : start + w, :] - quarters[q, :w, :] * scale
        span = pl.ds(start, w)
        stores.append(pltpu.make_async_copy(fresh_rows.at[span], new_rows.at[span], sems.at[q]))
        stores[-1].start()
    for store in stores:
        store.wait()


def update(me, pieces, rows, sums):
    return pl.pallas_call(
        update_body,
        in_specs=[SMEM] + [VMEM] * len(pieces) + [VMEM, VMEM],
        out_specs=[HBM, VMEM],
        out_shape=[
            jax.ShapeDtypeStruct(rows.shape, f32),
            jax.ShapeDtypeStruct(sums.shape, f32),
        ],
        scratch_shapes=[
            pltpu.VMEM((len(pieces), *pieces[0].shape), f32),
            pltpu.VMEM(rows.shape, f32),
            pltpu.SemaphoreType.DMA((len(pieces),)),
        ],
        compiler_params=room(16),
        name="update",
    )(me, *[near(piece) for piece in pieces], near(rows), sums)


def compact(slots, here, owners, capacity):
    half = capacity // 2
    who, k = slots // capacity, slots % capacity
    return jnp.where(k < half, who * half + k, owners * half + (who - here) % owners * half + k - half)


def local(embedding, adagrad_sum, row_lists, source_slots, target_slots, negative_ids):
    requests = row_lists[0, 0]
    owners, capacity = requests.shape
    half = capacity // 2
    rows = embedding.shape[0]
    groups = lax.axis_size("rep")
    edges = source_slots.shape[3]
    here = lax.axis_index("dom")
    given = exchanged(requests.reshape(owners, 1, capacity), "dom")
    incoming = given.reshape(owners, capacity)
    columns = embedding.T
    spread = spread_rows(columns)
    slots = jnp.stack([source_slots[0, 0], target_slots[0, 0]], axis=1).reshape(1, -1)
    slots = compact(slots, here, owners, capacity)
    live = owners * half + HEAVY * half
    padded = -(-live // LANES) * LANES
    plan = prep(slots, negative_ids[0, 0].reshape(1, -1), edges, live, padded)

    heads, tails = serve(given, here.reshape(1).astype(jnp.int32), spread)
    tails = tails.reshape(HEAVY, half, -1)
    tails = jnp.concatenate(
        [tails[0]] + [passed_along(tails[r], "dom", -r) for r in range(1, HEAVY)], axis=0
    )
    heads = exchanged(heads.reshape(owners, half, -1), "dom").reshape(owners * half, -1)
    me = lax.axis_index("rep")
    mine = me.reshape(1).astype(jnp.int32)
    askers = jnp.arange(owners)[None, :] == ((here - jnp.arange(HEAVY)) % owners)[:, None]
    tail_ids = jnp.sum(jnp.where(askers[:, :, None], incoming[None, :, half:], 0), axis=1)
    ids = jnp.concatenate([incoming[:, :half].reshape(1, -1), tail_ids.reshape(1, -1)], axis=1)
    listed = [ids] + [passed_along(ids, "rep", -s) for s in range(1, groups)]
    hot = hot_rows(mine, listed, rows)

    head_grads, tail_grads = grads(heads, tails, *plan, hot)
    tail_grads = tail_grads.reshape(HEAVY, half, -1)
    tail_grads = jnp.concatenate(
        [tail_grads[0]] + [passed_along(tail_grads[r], "dom", r) for r in range(1, HEAVY)], axis=0
    )
    tail_grads = jnp.moveaxis(tail_grads.reshape(HEAVY * half, groups, LANES), 1, 0)
    wanted = [
        lax.dynamic_index_in_dim(tail_grads, (me + groups - s) % groups, 0, keepdims=False)
        for s in range(groups)
    ]
    tail_back = jnp.concatenate(
        [wanted[0]] + [passed_along(wanted[s], "rep", -s) for s in range(1, groups)], axis=0
    )
    back = exchanged(head_grads.reshape(groups * owners, half, LANES), ("rep", "dom"))
    quarter = owner(back.reshape(-1, LANES), tail_back, hot)
    pieces = [quarter] + [passed_along(quarter, "rep", s) for s in range(1, len(WIDTHS))]
    new_rows, new_sums = update(mine, pieces, columns, adagrad_sum.reshape(1, -1))
    return new_rows.T, new_sums.reshape(-1)


def solution(mesh):
    in_specs = (
        P("dom", None),
        P("dom"),
        P("rep", "dom", None, None),
        P("rep", "dom", None, None),
        P("rep", "dom", None, None),
        P("rep", "dom", None, None, None),
    )
    out_specs = (P("dom", None), P("dom"))

    return jax.shard_map(local, mesh=mesh, in_specs=in_specs, out_specs=out_specs, check_vma=False)
```

```python
import jax
import jax.numpy as jnp
from jax import lax
from jax.experimental import pallas as pl
from jax.experimental.pallas import tpu as pltpu
from jax.sharding import PartitionSpec as P


HEAVY = 4
LEARN_RATE = 0.1
LANES = 128
MAIN = 104
SPARE = LANES - MAIN
QUARTERS = 4
f32 = jnp.float32
bf16 = jnp.bfloat16


def passed_along(value, axis, steps):
    count = lax.axis_size(axis)
    pairs = [(source, (source + steps) % count) for source in range(count)]
    return lax.ppermute(value, axis, pairs)


def exchanged(value, axis):
    return lax.all_to_all(value, axis, 0, 0, tiled=True)


def halves(x):
    high = x.astype(bf16)
    low = (x - high.astype(f32)).astype(bf16)
    return high, low


VMEM = pl.BlockSpec(memory_space=pltpu.VMEM)
SMEM = pl.BlockSpec(memory_space=pltpu.SMEM)
HBM = pl.BlockSpec(memory_space=pltpu.HBM)


def room(mib):
    return pltpu.CompilerParams(vmem_limit_bytes=mib << 20)


def far(x):
    return pltpu.with_memory_space_constraint(x, pltpu.HBM)


def near(x):
    return pltpu.with_memory_space_constraint(x, pltpu.VMEM)


def mm(a, b):
    return jnp.dot(a, b, preferred_element_type=f32)


def mm_nt(a, b):
    return lax.dot_general(a, b, (((1,), (1,)), ((), ())), preferred_element_type=f32)


def spread_body(columns, out):
    depth, rows = columns.shape
    for c in range(out.shape[1] // LANES):
        piece = columns[c * LANES : min((c + 1) * LANES, depth), :]
        if piece.shape[0] < LANES:
            piece = jnp.concatenate([piece, jnp.zeros((LANES - piece.shape[0], rows), f32)], axis=0)
        out[:, c * LANES : (c + 1) * LANES] = piece.T


def spread_rows(columns):
    return pl.pallas_call(
        spread_body,
        out_specs=VMEM,
        out_shape=pltpu.VMEM((columns.shape[1], LANES * QUARTERS), f32),
        compiler_params=room(16),
        name="spread",
    )(columns)


def serve_body(ids, here, rows, heads, tails, picked, ends, sems):
    owners = ids.shape[0]
    parts = sems.shape[0]
    each = owners // parts
    blocks = QUARTERS - 1
    tall = 8 * blocks + 1

    def eight(w, carry):
        taken = [rows[pl.ds(ids[w, 0, k], 1), :] for k in range(8)]
        for k in range(8):
            for c in range(blocks):
                picked[pl.ds(w * tall + 8 * c + k, 1), :] = taken[k][:, c * LANES : (c + 1) * LANES]
            ends[pl.ds(w * 8 + k, 1), :] = taken[k][:, blocks * LANES :]
        return carry

    for reach in range(HEAVY):
        asker = (here[0] + owners - reach) % owners
        for k in range(8):
            tails[reach * 8 + k : reach * 8 + k + 1, :] = rows[pl.ds(ids[asker, 0, 8 + k], 1), :]
    copies = []
    for part in range(parts):
        lax.fori_loop(part * each, (part + 1) * each, eight, 0, unroll=4)
        joined = ends[pl.ds(part * each * 8, each, stride=8), :]
        for k in range(1, 8):
            joined += pltpu.roll(ends[pl.ds(part * each * 8 + k, each, stride=8), :], 16 * k, 1)
        picked[pl.ds(part * each * tall + tall - 1, each, stride=tall), :] = joined
        span = pl.ds(part * each * tall, each * tall)
        copies.append(pltpu.make_async_copy(picked.at[span], heads.at[span], sems.at[part]))
        copies[-1].start()
    for copy in copies:
        copy.wait()


def serve(ids, here, rows):
    width = rows.shape[1]
    owners = ids.shape[0]
    shape = (owners * (8 * (QUARTERS - 1) + 1), LANES)
    return pl.pallas_call(
        serve_body,
        in_specs=[SMEM, SMEM, VMEM],
        out_specs=[HBM, VMEM],
        out_shape=[pltpu.HBM(shape, f32), jax.ShapeDtypeStruct((HEAVY * 8, width), f32)],
        scratch_shapes=[
            pltpu.VMEM(shape, f32),
            pltpu.VMEM((owners * 8, LANES), f32),
            pltpu.SemaphoreType.DMA((4,)),
        ],
        compiler_params=room(16),
        name="serve",
    )(ids, here, near(rows))


def prep_body(slots, negs, by_edge, by_slot, count_row, count_col):
    edges = count_row.shape[2]
    parts = slots.shape[1] // edges
    live = by_slot.shape[0]
    padded = by_edge.shape[1]
    one, zero = jnp.ones((), f32), jnp.zeros((), f32)
    for p in range(parts):
        row = slots[:, p * edges : (p + 1) * edges]
        down = lax.broadcasted_iota(jnp.int32, (live, edges), 0)
        by_slot[:, p * edges : (p + 1) * edges] = jnp.where(down == row, one, zero).astype(bf16)
        column = jnp.broadcast_to(row, (LANES, edges)).T
        across = lax.broadcasted_iota(jnp.int32, (edges, LANES), 1)
        for c in range(padded // LANES):
            by_edge[p * edges : (p + 1) * edges, c * LANES : (c + 1) * LANES] = jnp.where(
                across + c * LANES == column, one, zero
            ).astype(bf16)
        neg = negs[:, p * edges : (p + 1) * edges]
        down = lax.broadcasted_iota(jnp.int32, (edges, edges), 0)
        drawn = jnp.where(down == neg, one, zero).astype(bf16)
        if p % 2 == 0:
            count_row[p // 2] = mm_nt(jnp.ones((8, edges), bf16), drawn)
        else:
            count_col[p // 2] = mm(drawn, jnp.ones((edges, LANES), bf16))


def prep(slots, negs, edges, live, padded):
    total = slots.shape[1]
    batches = total // edges // 2
    return pl.pallas_call(
        prep_body,
        out_shape=[
            pltpu.HBM((total, padded), bf16),
            pltpu.HBM((live, total), bf16),
            pltpu.HBM((batches, 8, edges), f32),
            pltpu.HBM((batches, edges, LANES), f32),
        ],
        compiler_params=room(24),
        name="prep",
    )(slots, negs)


def lanes_of(shape):
    return lax.broadcasted_iota(jnp.int32, shape, 1)


def leftover(blocks):
    lane = lanes_of(blocks[0].shape)
    out = jnp.zeros(blocks[0].shape, f32)
    for c, block in enumerate(blocks):
        at = SPARE * c
        wide = SPARE if c < QUARTERS - 1 else 16
        moved = pltpu.roll(block, (at - (MAIN if c < QUARTERS - 1 else 0)) % LANES, 1)
        out = jnp.where((lane >= at) & (lane < at + wide), moved, out)
    return out


def grads_body(heads, tails, by_edge, by_slot, count_row, count_col, ahead, out_heads, out_tails,
               high, low, d_high, d_low, edge_part, slot_part, summed, packed, in_sems, out_sems):
    live = by_slot.shape[0]
    head_count = live - tails.shape[0]
    owners = head_count // 8
    tall = heads.shape[0] // owners
    padded = by_edge.shape[1]
    width = tails.shape[1]
    batches, _, edges = count_row.shape
    loads = []
    for p in range(2 * batches):
        span = pl.ds(p * edges, edges)
        loads.append(pltpu.make_async_copy(by_edge.at[span], edge_part.at[span], in_sems.at[p]))
        loads[-1].start()
    last = pltpu.make_async_copy(by_slot, slot_part, in_sems.at[2 * batches])
    last.start()
    ends = heads[pl.ds(tall - 1, owners, stride=tall), :]
    for k in range(8):
        span = slice(k * owners, (k + 1) * owners)
        for c in range(QUARTERS):
            lanes = slice(c * LANES, (c + 1) * LANES)
            if c < QUARTERS - 1:
                block = heads[pl.ds(8 * c + k, owners, stride=tall), :]
            else:
                block = pltpu.roll(ends, (LANES - 16 * k) % LANES, 1) if k else ends
                block = jnp.where(lanes_of(block.shape) < 16, block, 0.0)
            high[span, lanes], low[span, lanes] = halves(block)
    high[head_count:live, :], low[head_count:live, :] = halves(tails[...])
    high[live:, :] = jnp.zeros((padded - live, width), bf16)
    low[live:, :] = jnp.zeros((padded - live, width), bf16)
    for b in range(batches):
        picks = []
        for side in range(2):
            at = (2 * b + side) * edges
            loads[2 * b + side].wait()
            chosen = edge_part[at : at + edges, :]
            picks.append((mm(chosen, high[...]).astype(bf16), mm(chosen, low[...]).astype(bf16)))
        (s_high, s_low), (t_high, t_low) = picks
        scores = mm_nt(s_high, t_high) + mm_nt(s_high, t_low) + mm_nt(s_low, t_high)
        decay = jnp.exp(-jnp.abs(scores))
        upper = 1.0 / (1.0 + decay)
        lower = decay * upper
        sure = scores >= 0
        weight = jnp.where(sure, upper, lower)
        missing = jnp.where(sure, lower, upper)
        counts = count_row[b, 0:1, :] + jnp.concatenate([count_col[b]] * (edges // LANES), axis=1)
        down = lax.broadcasted_iota(jnp.int32, (edges, edges), 0)
        across = lax.broadcasted_iota(jnp.int32, (edges, edges), 1)
        gain = weight * counts * (1.0 / edges) - jnp.where(down == across, missing, 0.0)
        g_high, g_low = halves(gain)
        d_s = mm(g_high, t_high) + mm(g_high, t_low) + mm(g_low, t_high)
        at = 2 * b * edges
        d_high[at : at + edges, :], d_low[at : at + edges, :] = halves(d_s)
        g_high, g_low = halves(gain.T)
        d_t = mm(g_high, s_high) + mm(g_high, s_low) + mm(g_low, s_high)
        at += edges
        d_high[at : at + edges, :], d_low[at : at + edges, :] = halves(d_t)
    last.wait()
    stores = []
    block = 2 * LANES
    short = 7 * owners
    for h in range(width // block):
        span = slice(h * block, (h + 1) * block)
        summed[:, span] = mm(slot_part[...], d_high[:, span]) + mm(slot_part[...], d_low[:, span])
        for q in (2 * h, 2 * h + 1):

            def quarter(at, size):
                if q < QUARTERS - 1:
                    return summed[at : at + size, q * LANES : (q + 1) * LANES]
                return leftover([summed[at : at + size, c * LANES : (c + 1) * LANES] for c in range(QUARTERS)])

            eighth = quarter(7 * owners, owners)
            for k in range(7):
                value = quarter(k * owners, owners)
                if SPARE * k < MAIN:
                    moved = pltpu.roll(eighth, (MAIN - SPARE * k) % LANES, 1)
                    value = jnp.where(lanes_of(value.shape) < MAIN, value, moved)
                packed[pl.ds(q * short + k, owners, stride=7), :] = value
            out_tails[:, q * LANES : (q + 1) * LANES] = quarter(head_count, live - head_count)
        part = pl.ds(2 * h * short, 2 * short)
        stores.append(pltpu.make_async_copy(packed.at[part], out_heads.at[part], out_sems.at[h]))
        stores[-1].start()
    for store in stores:
        store.wait()


def grads(heads, tails, by_edge, by_slot, count_row, count_col, ahead):
    width = tails.shape[1]
    total, padded = by_edge.shape
    live = by_slot.shape[0]
    shape = (QUARTERS * 7 * (live - tails.shape[0]) // 8, LANES)
    return pl.pallas_call(
        grads_body,
        in_specs=[VMEM, VMEM, HBM, HBM, VMEM, VMEM, HBM],
        out_specs=[HBM, VMEM],
        out_shape=[pltpu.HBM(shape, f32), jax.ShapeDtypeStruct(tails.shape, f32)],
        scratch_shapes=[
            pltpu.VMEM((padded, width), bf16),
            pltpu.VMEM((padded, width), bf16),
            pltpu.VMEM((total, width), bf16),
            pltpu.VMEM((total, width), bf16),
            pltpu.VMEM(by_edge.shape, bf16),
            pltpu.VMEM(by_slot.shape, bf16),
            pltpu.VMEM((live, width), f32),
            pltpu.VMEM(shape, f32),
            pltpu.SemaphoreType.DMA((2 * count_row.shape[0] + 1,)),
            pltpu.SemaphoreType.DMA((width // LANES // 2,)),
        ],
        compiler_params=room(48),
        name="grads",
    )(near(heads), tails, far(by_edge), far(by_slot), count_row, count_col, far(ahead))


def hot_body(me, *refs):
    lists, hot = refs[:-1], refs[-1]
    rows = hot.shape[0]
    groups = len(lists)
    tail_count = HEAVY * 8
    head_count = lists[0].shape[1] - tail_count
    for s, ids in enumerate(lists):
        group = (me[0] + s) % groups
        down = lax.broadcasted_iota(jnp.int32, (rows, head_count), 0)
        spot = pl.multiple_of(group * head_count, LANES)
        hot[:, pl.ds(spot, head_count)] = jnp.where(down == ids[:, :head_count], 1.0, 0.0).astype(bf16)
    tails = jnp.concatenate([ids[:, head_count:] for ids in lists], axis=1)
    down = lax.broadcasted_iota(jnp.int32, (rows, tails.shape[1]), 0)
    hot[:, groups * head_count :] = jnp.where(down == tails, 1.0, 0.0).astype(bf16)


def hot_rows(me, lists, rows):
    vmem = pl.BlockSpec(memory_space=pltpu.VMEM)
    return pl.pallas_call(
        hot_body,
        in_specs=[pl.BlockSpec(memory_space=pltpu.SMEM)] + [vmem] * len(lists),
        out_shape=pltpu.HBM((rows, len(lists) * lists[0].shape[1]), bf16),
        compiler_params=room(16),
        name="hot",
    )(me, *lists)


def owner_body(back, tails, hot, out, spots, sems):
    parts = sems.shape[0] - 1
    short = back.shape[0] // parts
    each = short // 7 * 8
    owners = short // 7
    spans = [(p * each, each) for p in range(parts)] + [(parts * each, tails.shape[0])]
    loads = []
    for p, (at, size) in enumerate(spans):
        loads.append(pltpu.make_async_copy(hot.at[:, pl.ds(at, size)], spots.at[:, pl.ds(at, size)], sems.at[p]))
        loads[-1].start()
    summed = jnp.zeros((hot.shape[0], LANES), f32)
    for p, (at, size) in enumerate(spans):
        if p < parts:
            eighth = jnp.zeros((owners, LANES), f32)
            lane = lanes_of(eighth.shape)
            for k in range(-(-MAIN // SPARE)):
                moved = pltpu.roll(back[pl.ds(p * short + k, owners, stride=7), :], (SPARE * k - MAIN) % LANES, 1)
                eighth = jnp.where((lane >= SPARE * k) & (lane < SPARE * (k + 1)), moved, eighth)
            values = jnp.concatenate([back[p * short : (p + 1) * short, :], eighth], axis=0)
        else:
            values = tails[...]
        both = jnp.concatenate(halves(values), axis=1)
        loads[p].wait()
        part = mm(spots[:, at : at + size], both)
        summed += part[:, :LANES] + part[:, LANES:]
    out[...] = summed.T[: out.shape[0], :]


def owner(back, tails, hot):
    return pl.pallas_call(
        owner_body,
        in_specs=[VMEM, VMEM, HBM],
        out_specs=VMEM,
        out_shape=jax.ShapeDtypeStruct((MAIN, hot.shape[0]), f32),
        scratch_shapes=[pltpu.VMEM(hot.shape, bf16), pltpu.SemaphoreType.DMA((5,))],
        compiler_params=room(16),
        name="owner",
    )(near(back), tails, far(hot))


def update_body(me, own, next1, next2, next3, rows, sums, new_rows, new_sums, quarters, fresh_rows, sems):
    for s, piece in enumerate((own, next1, next2, next3)):
        quarters[(me[0] + 4 - s) % 4] = piece[...]
    squares = jnp.zeros(sums.shape, f32)
    for q in range(QUARTERS):
        squares += jnp.sum(quarters[q] * quarters[q], axis=0, keepdims=True)
    fresh = sums[...] + squares * (1.0 / rows.shape[0])
    new_sums[...] = fresh
    scale = LEARN_RATE / jnp.sqrt(fresh)
    depth = rows.shape[0]
    stores = []
    for c in range(QUARTERS - 1):
        at = c * LANES
        end = at + LANES
        wide = SPARE
        if c == QUARTERS - 2:
            end = depth
            wide = depth - at - MAIN
        main = slice(at, at + MAIN)
        rest = slice(at + MAIN, end)
        fresh_rows[main, :] = rows[main, :] - quarters[c] * scale
        fresh_rows[rest, :] = rows[rest, :] - quarters[QUARTERS - 1, SPARE * c : SPARE * c + wide, :] * scale
        span = pl.ds(at, end - at)
        stores.append(pltpu.make_async_copy(fresh_rows.at[span], new_rows.at[span], sems.at[c]))
        stores[-1].start()
    for store in stores:
        store.wait()


def update(me, pieces, rows, sums):
    return pl.pallas_call(
        update_body,
        in_specs=[SMEM] + [VMEM] * len(pieces) + [VMEM, VMEM],
        out_specs=[HBM, VMEM],
        out_shape=[
            jax.ShapeDtypeStruct(rows.shape, f32),
            jax.ShapeDtypeStruct(sums.shape, f32),
        ],
        scratch_shapes=[
            pltpu.VMEM((len(pieces), *pieces[0].shape), f32),
            pltpu.VMEM(rows.shape, f32),
            pltpu.SemaphoreType.DMA((len(pieces),)),
        ],
        compiler_params=room(16),
        name="update",
    )(me, *[near(piece) for piece in pieces], near(rows), sums)


def compact(slots, here, owners, capacity):
    half = capacity // 2
    who, k = slots // capacity, slots % capacity
    return jnp.where(k < half, k * owners + who, owners * half + (who - here) % owners * half + k - half)


def local(embedding, adagrad_sum, row_lists, source_slots, target_slots, negative_ids):
    requests = row_lists[0, 0]
    owners, capacity = requests.shape
    half = capacity // 2
    rows = embedding.shape[0]
    groups = lax.axis_size("rep")
    edges = source_slots.shape[3]
    here = lax.axis_index("dom")
    given = exchanged(requests.reshape(owners, 1, capacity), "dom")
    incoming = given.reshape(owners, capacity)
    columns = embedding.T
    spread = spread_rows(columns)
    slots = jnp.stack([source_slots[0, 0], target_slots[0, 0]], axis=1).reshape(1, -1)
    slots = compact(slots, here, owners, capacity)
    live = owners * half + HEAVY * half
    padded = -(-live // LANES) * LANES
    plan = prep(slots, negative_ids[0, 0].reshape(1, -1), edges, live, padded)

    heads, tails = serve(given, here.reshape(1).astype(jnp.int32), spread)
    tails = tails.reshape(HEAVY, half, -1)
    tails = jnp.concatenate(
        [tails[0]] + [passed_along(tails[r], "dom", -r) for r in range(1, HEAVY)], axis=0
    )
    heads = exchanged(heads.reshape(owners, -1, 1, LANES), "dom").reshape(-1, LANES)
    me = lax.axis_index("rep")
    mine = me.reshape(1).astype(jnp.int32)
    askers = jnp.arange(owners)[None, :] == ((here - jnp.arange(HEAVY)) % owners)[:, None]
    tail_ids = jnp.sum(jnp.where(askers[:, :, None], incoming[None, :, half:], 0), axis=1)
    ids = [incoming[:, : half - 1], incoming[:, half - 1], tail_ids]
    ids = jnp.concatenate([part.reshape(1, -1) for part in ids], axis=1)
    listed = [ids] + [passed_along(ids, "rep", -s) for s in range(1, groups)]
    hot = hot_rows(mine, listed, rows)

    head_grads, tail_grads = grads(heads, tails, *plan, hot)
    tail_grads = tail_grads.reshape(HEAVY, half, -1)
    tail_grads = jnp.concatenate(
        [tail_grads[0]] + [passed_along(tail_grads[r], "dom", r) for r in range(1, HEAVY)], axis=0
    )
    tail_grads = jnp.moveaxis(tail_grads.reshape(HEAVY * half, groups, LANES), 1, 0)
    wanted = [
        lax.dynamic_index_in_dim(tail_grads, (me + groups - s) % groups, 0, keepdims=False)
        for s in range(groups)
    ]
    tail_back = jnp.concatenate(
        [wanted[0]] + [passed_along(wanted[s], "rep", -s) for s in range(1, groups)], axis=0
    )
    back = exchanged(head_grads.reshape(groups * owners, half - 1, 1, LANES), ("rep", "dom"))
    quarter = owner(back.reshape(-1, LANES), tail_back, hot)
    pieces = [quarter] + [passed_along(quarter, "rep", s) for s in range(1, groups)]
    new_rows, new_sums = update(mine, pieces, columns, adagrad_sum.reshape(1, -1))
    return new_rows.T, new_sums.reshape(-1)


def solution(mesh):
    in_specs = (
        P("dom", None),
        P("dom"),
        P("rep", "dom", None, None),
        P("rep", "dom", None, None),
        P("rep", "dom", None, None),
        P("rep", "dom", None, None, None),
    )
    out_specs = (P("dom", None), P("dom"))

    return jax.shard_map(local, mesh=mesh, in_specs=in_specs, out_specs=out_specs, check_vma=False)
```

```python
import jax
import jax.numpy as jnp
from jax import lax
from jax.experimental import pallas as pl
from jax.experimental.pallas import tpu as pltpu
from jax.sharding import PartitionSpec as P


HEAVY = 4
LEARN_RATE = 0.1
LANES = 128
MAIN = 104
SPARE = LANES - MAIN
QUARTERS = 4
f32 = jnp.float32
bf16 = jnp.bfloat16


def passed_along(value, axis, steps):
    count = lax.axis_size(axis)
    pairs = [(source, (source + steps) % count) for source in range(count)]
    return lax.ppermute(value, axis, pairs)


def exchanged(value, axis):
    return lax.all_to_all(value, axis, 0, 0, tiled=True)


def halves(x):
    high = x.astype(bf16)
    low = (x - high.astype(f32)).astype(bf16)
    return high, low


VMEM = pl.BlockSpec(memory_space=pltpu.VMEM)
SMEM = pl.BlockSpec(memory_space=pltpu.SMEM)
HBM = pl.BlockSpec(memory_space=pltpu.HBM)


def room(mib):
    return pltpu.CompilerParams(vmem_limit_bytes=mib << 20)


def far(x):
    return pltpu.with_memory_space_constraint(x, pltpu.HBM)


def near(x):
    return pltpu.with_memory_space_constraint(x, pltpu.VMEM)


def mm(a, b):
    return jnp.dot(a, b, preferred_element_type=f32)


def mm_nt(a, b):
    return lax.dot_general(a, b, (((1,), (1,)), ((), ())), preferred_element_type=f32)


def spread_body(columns, out):
    depth, rows = columns.shape
    for c in range(out.shape[1] // LANES):
        piece = columns[c * LANES : min((c + 1) * LANES, depth), :]
        if piece.shape[0] < LANES:
            piece = jnp.concatenate([piece, jnp.zeros((LANES - piece.shape[0], rows), f32)], axis=0)
        out[:, c * LANES : (c + 1) * LANES] = piece.T


def spread_rows(columns):
    return pl.pallas_call(
        spread_body,
        out_specs=VMEM,
        out_shape=pltpu.VMEM((columns.shape[1], LANES * QUARTERS), f32),
        compiler_params=room(16),
        name="spread",
    )(columns)


def serve_body(ids, here, rows, heads, tails, picked, ends, sems):
    owners = ids.shape[0]
    parts = sems.shape[0]
    each = owners // parts
    blocks = QUARTERS - 1
    tall = 8 * blocks + 1

    def eight(w, carry):
        taken = [rows[pl.ds(ids[w, 0, k], 1), :] for k in range(8)]
        for k in range(8):
            for c in range(blocks):
                picked[pl.ds(w * tall + 8 * c + k, 1), :] = taken[k][:, c * LANES : (c + 1) * LANES]
            ends[pl.ds(w * 8 + k, 1), :] = taken[k][:, blocks * LANES :]
        return carry

    for reach in range(HEAVY):
        asker = (here[0] + owners - reach) % owners
        for k in range(8):
            tails[reach * 8 + k : reach * 8 + k + 1, :] = rows[pl.ds(ids[asker, 0, 8 + k], 1), :]
    copies = []
    for part in range(parts):
        lax.fori_loop(part * each, (part + 1) * each, eight, 0, unroll=4)
        joined = ends[pl.ds(part * each * 8, each, stride=8), :]
        for k in range(1, 8):
            joined += pltpu.roll(ends[pl.ds(part * each * 8 + k, each, stride=8), :], 16 * k, 1)
        picked[pl.ds(part * each * tall + tall - 1, each, stride=tall), :] = joined
        span = pl.ds(part * each * tall, each * tall)
        copies.append(pltpu.make_async_copy(picked.at[span], heads.at[span], sems.at[part]))
        copies[-1].start()
    for copy in copies:
        copy.wait()


def serve(ids, here, rows):
    width = rows.shape[1]
    owners = ids.shape[0]
    shape = (owners * (8 * (QUARTERS - 1) + 1), LANES)
    return pl.pallas_call(
        serve_body,
        in_specs=[SMEM, SMEM, VMEM],
        out_specs=[HBM, VMEM],
        out_shape=[pltpu.HBM(shape, f32), jax.ShapeDtypeStruct((HEAVY * 8, width), f32)],
        scratch_shapes=[
            pltpu.VMEM(shape, f32),
            pltpu.VMEM((owners * 8, LANES), f32),
            pltpu.SemaphoreType.DMA((4,)),
        ],
        compiler_params=room(16),
        name="serve",
    )(ids, here, near(rows))


def prep_body(slots, negs, by_edge, by_slot, count_row, count_col):
    edges = count_row.shape[2]
    parts = slots.shape[1] // edges
    live = by_slot.shape[0]
    padded = by_edge.shape[1]
    one, zero = jnp.ones((), f32), jnp.zeros((), f32)
    for p in range(parts):
        row = slots[:, p * edges : (p + 1) * edges]
        down = lax.broadcasted_iota(jnp.int32, (live, edges), 0)
        by_slot[:, p * edges : (p + 1) * edges] = jnp.where(down == row, one, zero).astype(bf16)
        column = jnp.broadcast_to(row, (LANES, edges)).T
        across = lax.broadcasted_iota(jnp.int32, (edges, LANES), 1)
        for c in range(padded // LANES):
            by_edge[p * edges : (p + 1) * edges, c * LANES : (c + 1) * LANES] = jnp.where(
                across + c * LANES == column, one, zero
            ).astype(bf16)
        neg = negs[:, p * edges : (p + 1) * edges]
        down = lax.broadcasted_iota(jnp.int32, (edges, edges), 0)
        drawn = jnp.where(down == neg, one, zero).astype(bf16)
        if p % 2 == 0:
            count_row[p // 2] = mm_nt(jnp.ones((8, edges), bf16), drawn)
        else:
            count_col[p // 2] = mm(drawn, jnp.ones((edges, LANES), bf16))


def prep(slots, negs, edges, live, padded):
    total = slots.shape[1]
    batches = total // edges // 2
    return pl.pallas_call(
        prep_body,
        out_shape=[
            pltpu.HBM((total, padded), bf16),
            pltpu.HBM((live, total), bf16),
            pltpu.HBM((batches, 8, edges), f32),
            pltpu.HBM((batches, edges, LANES), f32),
        ],
        compiler_params=room(24),
        name="prep",
    )(slots, negs)


def lanes_of(shape):
    return lax.broadcasted_iota(jnp.int32, shape, 1)


def leftover(blocks):
    lane = lanes_of(blocks[0].shape)
    out = jnp.zeros(blocks[0].shape, f32)
    for c, block in enumerate(blocks):
        at = SPARE * c
        wide = SPARE if c < QUARTERS - 1 else 16
        moved = pltpu.roll(block, (at - (MAIN if c < QUARTERS - 1 else 0)) % LANES, 1)
        out = jnp.where((lane >= at) & (lane < at + wide), moved, out)
    return out


def grads_body(heads, tails, by_edge, by_slot, count_row, count_col, ahead, out_heads, out_tails,
               high, low, d_high, d_low, edge_part, slot_part, summed, packed, in_sems, out_sems):
    live = by_slot.shape[0]
    head_count = live - tails.shape[0]
    owners = head_count // 8
    tall = heads.shape[0] // owners
    padded = by_edge.shape[1]
    width = tails.shape[1]
    batches, _, edges = count_row.shape
    loads = []
    for p in range(2 * batches):
        span = pl.ds(p * edges, edges)
        loads.append(pltpu.make_async_copy(by_edge.at[span], edge_part.at[span], in_sems.at[p]))
        loads[-1].start()
    last = pltpu.make_async_copy(by_slot, slot_part, in_sems.at[2 * batches])
    last.start()
    ends = heads[pl.ds(tall - 1, owners, stride=tall), :]
    for k in range(8):
        span = slice(k * owners, (k + 1) * owners)
        for c in range(QUARTERS):
            lanes = slice(c * LANES, (c + 1) * LANES)
            if c < QUARTERS - 1:
                block = heads[pl.ds(8 * c + k, owners, stride=tall), :]
            else:
                block = pltpu.roll(ends, (LANES - 16 * k) % LANES, 1) if k else ends
                block = jnp.where(lanes_of(block.shape) < 16, block, 0.0)
            high[span, lanes], low[span, lanes] = halves(block)
    high[head_count:live, :], low[head_count:live, :] = halves(tails[...])
    high[live:, :] = jnp.zeros((padded - live, width), bf16)
    low[live:, :] = jnp.zeros((padded - live, width), bf16)

    def gathered(b):
        picks = []
        for side in range(2):
            at = (2 * b + side) * edges
            loads[2 * b + side].wait()
            chosen = edge_part[at : at + edges, :]
            picks.append((mm(chosen, high[...]).astype(bf16), mm(chosen, low[...]).astype(bf16)))
        return picks

    def scored(picks):
        (s_high, s_low), (t_high, t_low) = picks
        return mm_nt(s_high, t_high) + mm_nt(s_high, t_low) + mm_nt(s_low, t_high)

    def gained(b, scores):
        decay = jnp.exp(-jnp.abs(scores))
        upper = 1.0 / (1.0 + decay)
        lower = decay * upper
        sure = scores >= 0
        weight = jnp.where(sure, upper, lower)
        missing = jnp.where(sure, lower, upper)
        counts = count_row[b, 0:1, :] + jnp.concatenate([count_col[b]] * (edges // LANES), axis=1)
        down = lax.broadcasted_iota(jnp.int32, (edges, edges), 0)
        across = lax.broadcasted_iota(jnp.int32, (edges, edges), 1)
        return weight * counts * (1.0 / edges) - jnp.where(down == across, missing, 0.0)

    def pulled(at, gain, high_rows, low_rows):
        g_high, g_low = halves(gain)
        moved = mm(g_high, high_rows) + mm(g_high, low_rows) + mm(g_low, high_rows)
        d_high[at : at + edges, :], d_low[at : at + edges, :] = halves(moved)

    picks = gathered(0)
    scores = scored(picks)
    for b in range(batches):
        if b + 1 < batches:
            next_picks = gathered(b + 1)
        gain = gained(b, scores)
        if b + 1 < batches:
            next_scores = scored(next_picks)
        pulled(2 * b * edges, gain, *picks[1])
        pulled((2 * b + 1) * edges, gain.T, *picks[0])
        if b + 1 < batches:
            picks, scores = next_picks, next_scores
    last.wait()
    stores = []
    block = 2 * LANES
    short = 7 * owners
    for h in range(width // block):
        span = slice(h * block, (h + 1) * block)
        summed[:, span] = mm(slot_part[...], d_high[:, span]) + mm(slot_part[...], d_low[:, span])
        for q in (2 * h, 2 * h + 1):

            def quarter(at, size):
                if q < QUARTERS - 1:
                    return summed[at : at + size, q * LANES : (q + 1) * LANES]
                return leftover([summed[at : at + size, c * LANES : (c + 1) * LANES] for c in range(QUARTERS)])

            eighth = quarter(7 * owners, owners)
            for k in range(7):
                value = quarter(k * owners, owners)
                if SPARE * k < MAIN:
                    moved = pltpu.roll(eighth, (MAIN - SPARE * k) % LANES, 1)
                    value = jnp.where(lanes_of(value.shape) < MAIN, value, moved)
                packed[pl.ds(q * short + k, owners, stride=7), :] = value
            out_tails[:, q * LANES : (q + 1) * LANES] = quarter(head_count, live - head_count)
        part = pl.ds(2 * h * short, 2 * short)
        stores.append(pltpu.make_async_copy(packed.at[part], out_heads.at[part], out_sems.at[h]))
        stores[-1].start()
    for store in stores:
        store.wait()


def grads(heads, tails, by_edge, by_slot, count_row, count_col, ahead):
    width = tails.shape[1]
    total, padded = by_edge.shape
    live = by_slot.shape[0]
    shape = (QUARTERS * 7 * (live - tails.shape[0]) // 8, LANES)
    return pl.pallas_call(
        grads_body,
        in_specs=[VMEM, VMEM, HBM, HBM, VMEM, VMEM, HBM],
        out_specs=[HBM, VMEM],
        out_shape=[pltpu.HBM(shape, f32), jax.ShapeDtypeStruct(tails.shape, f32)],
        scratch_shapes=[
            pltpu.VMEM((padded, width), bf16),
            pltpu.VMEM((padded, width), bf16),
            pltpu.VMEM((total, width), bf16),
            pltpu.VMEM((total, width), bf16),
            pltpu.VMEM(by_edge.shape, bf16),
            pltpu.VMEM(by_slot.shape, bf16),
            pltpu.VMEM((live, width), f32),
            pltpu.VMEM(shape, f32),
            pltpu.SemaphoreType.DMA((2 * count_row.shape[0] + 1,)),
            pltpu.SemaphoreType.DMA((width // LANES // 2,)),
        ],
        compiler_params=room(48),
        name="grads",
    )(near(heads), tails, far(by_edge), far(by_slot), count_row, count_col, far(ahead))


def hot_body(me, *refs):
    lists, hot = refs[:-1], refs[-1]
    rows = hot.shape[0]
    groups = len(lists)
    tail_count = HEAVY * 8
    head_count = lists[0].shape[1] - tail_count
    for s, ids in enumerate(lists):
        group = (me[0] + s) % groups
        down = lax.broadcasted_iota(jnp.int32, (rows, head_count), 0)
        spot = pl.multiple_of(group * head_count, LANES)
        hot[:, pl.ds(spot, head_count)] = jnp.where(down == ids[:, :head_count], 1.0, 0.0).astype(bf16)
    tails = jnp.concatenate([ids[:, head_count:] for ids in lists], axis=1)
    down = lax.broadcasted_iota(jnp.int32, (rows, tails.shape[1]), 0)
    hot[:, groups * head_count :] = jnp.where(down == tails, 1.0, 0.0).astype(bf16)


def hot_rows(me, lists, rows):
    vmem = pl.BlockSpec(memory_space=pltpu.VMEM)
    return pl.pallas_call(
        hot_body,
        in_specs=[pl.BlockSpec(memory_space=pltpu.SMEM)] + [vmem] * len(lists),
        out_shape=pltpu.HBM((rows, len(lists) * lists[0].shape[1]), bf16),
        compiler_params=room(16),
        name="hot",
    )(me, *lists)


def owner_body(back, tails, hot, out, spots, sems):
    parts = sems.shape[0] - 1
    short = back.shape[0] // parts
    each = short // 7 * 8
    owners = short // 7
    spans = [(p * each, each) for p in range(parts)] + [(parts * each, tails.shape[0])]
    loads = []
    for p, (at, size) in enumerate(spans):
        loads.append(pltpu.make_async_copy(hot.at[:, pl.ds(at, size)], spots.at[:, pl.ds(at, size)], sems.at[p]))
        loads[-1].start()
    summed = jnp.zeros((hot.shape[0], LANES), f32)
    for p, (at, size) in enumerate(spans):
        if p < parts:
            eighth = jnp.zeros((owners, LANES), f32)
            lane = lanes_of(eighth.shape)
            for k in range(-(-MAIN // SPARE)):
                moved = pltpu.roll(back[pl.ds(p * short + k, owners, stride=7), :], (SPARE * k - MAIN) % LANES, 1)
                eighth = jnp.where((lane >= SPARE * k) & (lane < SPARE * (k + 1)), moved, eighth)
            values = jnp.concatenate([back[p * short : (p + 1) * short, :], eighth], axis=0)
        else:
            values = tails[...]
        both = jnp.concatenate(halves(values), axis=1)
        loads[p].wait()
        part = mm(spots[:, at : at + size], both)
        summed += part[:, :LANES] + part[:, LANES:]
    out[...] = summed.T[: out.shape[0], :]


def owner(back, tails, hot):
    return pl.pallas_call(
        owner_body,
        in_specs=[VMEM, VMEM, HBM],
        out_specs=VMEM,
        out_shape=jax.ShapeDtypeStruct((MAIN, hot.shape[0]), f32),
        scratch_shapes=[pltpu.VMEM(hot.shape, bf16), pltpu.SemaphoreType.DMA((5,))],
        compiler_params=room(16),
        name="owner",
    )(near(back), tails, far(hot))


def update_body(me, own, next1, next2, next3, rows, sums, new_rows, new_sums, quarters, fresh_rows, sems):
    for s, piece in enumerate((own, next1, next2, next3)):
        quarters[(me[0] + 4 - s) % 4] = piece[...]
    squares = jnp.zeros(sums.shape, f32)
    for q in range(QUARTERS):
        squares += jnp.sum(quarters[q] * quarters[q], axis=0, keepdims=True)
    fresh = sums[...] + squares * (1.0 / rows.shape[0])
    new_sums[...] = fresh
    scale = LEARN_RATE / jnp.sqrt(fresh)
    depth = rows.shape[0]
    stores = []
    for c in range(QUARTERS - 1):
        at = c * LANES
        end = at + LANES
        wide = SPARE
        if c == QUARTERS - 2:
            end = depth
            wide = depth - at - MAIN
        main = slice(at, at + MAIN)
        rest = slice(at + MAIN, end)
        fresh_rows[main, :] = rows[main, :] - quarters[c] * scale
        fresh_rows[rest, :] = rows[rest, :] - quarters[QUARTERS - 1, SPARE * c : SPARE * c + wide, :] * scale
        span = pl.ds(at, end - at)
        stores.append(pltpu.make_async_copy(fresh_rows.at[span], new_rows.at[span], sems.at[c]))
        stores[-1].start()
    for store in stores:
        store.wait()


def update(me, pieces, rows, sums):
    return pl.pallas_call(
        update_body,
        in_specs=[SMEM] + [VMEM] * len(pieces) + [VMEM, VMEM],
        out_specs=[HBM, VMEM],
        out_shape=[
            jax.ShapeDtypeStruct(rows.shape, f32),
            jax.ShapeDtypeStruct(sums.shape, f32),
        ],
        scratch_shapes=[
            pltpu.VMEM((len(pieces), *pieces[0].shape), f32),
            pltpu.VMEM(rows.shape, f32),
            pltpu.SemaphoreType.DMA((len(pieces),)),
        ],
        compiler_params=room(16),
        name="update",
    )(me, *[near(piece) for piece in pieces], near(rows), sums)


def compact(slots, here, owners, capacity):
    half = capacity // 2
    who, k = slots // capacity, slots % capacity
    return jnp.where(k < half, k * owners + who, owners * half + (who - here) % owners * half + k - half)


def local(embedding, adagrad_sum, row_lists, source_slots, target_slots, negative_ids):
    requests = row_lists[0, 0]
    owners, capacity = requests.shape
    half = capacity // 2
    rows = embedding.shape[0]
    groups = lax.axis_size("rep")
    edges = source_slots.shape[3]
    here = lax.axis_index("dom")
    given = exchanged(requests.reshape(owners, 1, capacity), "dom")
    incoming = given.reshape(owners, capacity)
    columns = embedding.T
    spread = spread_rows(columns)
    slots = jnp.stack([source_slots[0, 0], target_slots[0, 0]], axis=1).reshape(1, -1)
    slots = compact(slots, here, owners, capacity)
    live = owners * half + HEAVY * half
    padded = -(-live // LANES) * LANES
    plan = prep(slots, negative_ids[0, 0].reshape(1, -1), edges, live, padded)

    heads, tails = serve(given, here.reshape(1).astype(jnp.int32), spread)
    tails = tails.reshape(HEAVY, half, -1)
    tails = jnp.concatenate(
        [tails[0]] + [passed_along(tails[r], "dom", -r) for r in range(1, HEAVY)], axis=0
    )
    heads = exchanged(heads.reshape(owners, -1, 1, LANES), "dom").reshape(-1, LANES)
    me = lax.axis_index("rep")
    mine = me.reshape(1).astype(jnp.int32)
    askers = jnp.arange(owners)[None, :] == ((here - jnp.arange(HEAVY)) % owners)[:, None]
    tail_ids = jnp.sum(jnp.where(askers[:, :, None], incoming[None, :, half:], 0), axis=1)
    ids = [incoming[:, : half - 1], incoming[:, half - 1], tail_ids]
    ids = jnp.concatenate([part.reshape(1, -1) for part in ids], axis=1)
    listed = [ids] + [passed_along(ids, "rep", -s) for s in range(1, groups)]
    hot = hot_rows(mine, listed, rows)

    head_grads, tail_grads = grads(heads, tails, *plan, hot)
    back = exchanged(head_grads.reshape(groups * owners, half - 1, 1, LANES), ("rep", "dom"))
    tail_grads = jnp.moveaxis(tail_grads.reshape(HEAVY * half, groups, LANES), 1, 0)
    wanted = [
        lax.dynamic_index_in_dim(tail_grads, (me + groups - s) % groups, 0, keepdims=False)
        for s in range(groups)
    ]
    tail_grads = jnp.stack(
        [wanted[0]] + [passed_along(wanted[s], "rep", -s) for s in range(1, groups)], axis=0
    ).reshape(groups, HEAVY, half, LANES)
    tail_back = [tail_grads[:, 0]] + [passed_along(tail_grads[:, r], "dom", r) for r in range(1, HEAVY)]
    tail_back = jnp.stack(tail_back, axis=1).reshape(-1, LANES)
    quarter = owner(back.reshape(-1, LANES), tail_back, hot)
    pieces = [quarter] + [passed_along(quarter, "rep", s) for s in range(1, groups)]
    new_rows, new_sums = update(mine, pieces, columns, adagrad_sum.reshape(1, -1))
    return new_rows.T, new_sums.reshape(-1)


def solution(mesh):
    in_specs = (
        P("dom", None),
        P("dom"),
        P("rep", "dom", None, None),
        P("rep", "dom", None, None),
        P("rep", "dom", None, None),
        P("rep", "dom", None, None, None),
    )
    out_specs = (P("dom", None), P("dom"))

    return jax.shard_map(local, mesh=mesh, in_specs=in_specs, out_specs=out_specs, check_vma=False)
```

```python
import jax
import jax.numpy as jnp
from jax import lax
from jax.experimental import pallas as pl
from jax.experimental.pallas import tpu as pltpu
from jax.sharding import PartitionSpec as P


HEAVY = 4
LEARN_RATE = 0.1
LOG2E = 1.4426950408889634
LANES = 128
MAIN = 104
SPARE = LANES - MAIN
QUARTERS = 4
f32 = jnp.float32
bf16 = jnp.bfloat16


def passed_along(value, axis, steps):
    count = lax.axis_size(axis)
    pairs = [(source, (source + steps) % count) for source in range(count)]
    return lax.ppermute(value, axis, pairs)


def exchanged(value, axis):
    return lax.all_to_all(value, axis, 0, 0, tiled=True)


def halves(x):
    high = x.astype(bf16)
    low = (x - high.astype(f32)).astype(bf16)
    return high, low


VMEM = pl.BlockSpec(memory_space=pltpu.VMEM)
SMEM = pl.BlockSpec(memory_space=pltpu.SMEM)
HBM = pl.BlockSpec(memory_space=pltpu.HBM)


def room(mib):
    return pltpu.CompilerParams(vmem_limit_bytes=mib << 20)


def far(x):
    return pltpu.with_memory_space_constraint(x, pltpu.HBM)


def near(x):
    return pltpu.with_memory_space_constraint(x, pltpu.VMEM)


def mm(a, b):
    return jnp.dot(a, b, preferred_element_type=f32)


def mm_nt(a, b):
    return lax.dot_general(a, b, (((1,), (1,)), ((), ())), preferred_element_type=f32)


def spread_body(columns, out):
    depth, rows = columns.shape
    for c in range(out.shape[1]):
        piece = columns[c * LANES : min((c + 1) * LANES, depth), :]
        if piece.shape[0] < LANES:
            piece = jnp.concatenate([piece, jnp.zeros((LANES - piece.shape[0], rows), f32)], axis=0)
        out[:, c, :] = piece.T


def spread_rows(columns):
    return pl.pallas_call(
        spread_body,
        out_specs=VMEM,
        out_shape=pltpu.VMEM((columns.shape[1], QUARTERS, LANES), f32),
        compiler_params=room(16),
        name="spread",
    )(columns)


def serve_body(ids, here, rows, heads, tails, picked, ends, sems):
    owners = ids.shape[0]
    parts = sems.shape[0]
    each = owners // parts
    blocks = QUARTERS - 1
    tall = 8 * blocks + 1

    def eight(w, carry):
        taken = [rows[ids[w, 0, k]] for k in range(8)]
        for k in range(8):
            picked[pl.ds(w * tall + k, blocks, stride=8), :] = taken[k][:blocks]
            ends[pl.ds(w * 8 + k, 1), :] = taken[k][blocks:]
        return carry

    for reach in range(HEAVY):
        asker = (here[0] + owners - reach) % owners
        for k in range(8):
            row = rows[ids[asker, 0, 8 + k]]
            for c in range(QUARTERS):
                tails[reach * 8 + k : reach * 8 + k + 1, c * LANES : (c + 1) * LANES] = row[c : c + 1]
    copies = []
    for part in range(parts):
        lax.fori_loop(part * each, (part + 1) * each, eight, 0, unroll=4)
        joined = ends[pl.ds(part * each * 8, each, stride=8), :]
        for k in range(1, 8):
            joined += pltpu.roll(ends[pl.ds(part * each * 8 + k, each, stride=8), :], 16 * k, 1)
        picked[pl.ds(part * each * tall + tall - 1, each, stride=tall), :] = joined
        span = pl.ds(part * each * tall, each * tall)
        copies.append(pltpu.make_async_copy(picked.at[span], heads.at[span], sems.at[part]))
        copies[-1].start()
    for copy in copies:
        copy.wait()


def serve(ids, here, rows):
    width = QUARTERS * LANES
    owners = ids.shape[0]
    shape = (owners * (8 * (QUARTERS - 1) + 1), LANES)
    return pl.pallas_call(
        serve_body,
        in_specs=[SMEM, SMEM, VMEM],
        out_specs=[HBM, VMEM],
        out_shape=[pltpu.HBM(shape, f32), jax.ShapeDtypeStruct((HEAVY * 8, width), f32)],
        scratch_shapes=[
            pltpu.VMEM(shape, f32),
            pltpu.VMEM((owners * 8, LANES), f32),
            pltpu.SemaphoreType.DMA((4,)),
        ],
        compiler_params=room(16),
        name="serve",
    )(ids, here, near(rows))


def prep_body(slots, negs, by_edge, by_slot, count_row, count_col):
    edges = count_row.shape[2]
    parts = slots.shape[1] // edges
    live = by_slot.shape[0]
    padded = by_edge.shape[1]
    one, zero = jnp.ones((), f32), jnp.zeros((), f32)
    for p in range(parts):
        row = slots[:, p * edges : (p + 1) * edges]
        down = lax.broadcasted_iota(jnp.int32, (live, edges), 0)
        by_slot[:, p * edges : (p + 1) * edges] = jnp.where(down == row, one, zero).astype(bf16)
        column = jnp.broadcast_to(row, (LANES, edges)).T
        across = lax.broadcasted_iota(jnp.int32, (edges, LANES), 1)
        for c in range(padded // LANES):
            by_edge[p * edges : (p + 1) * edges, c * LANES : (c + 1) * LANES] = jnp.where(
                across + c * LANES == column, one, zero
            ).astype(bf16)
        neg = negs[:, p * edges : (p + 1) * edges]
        down = lax.broadcasted_iota(jnp.int32, (edges, edges), 0)
        drawn = jnp.where(down == neg, one, zero).astype(bf16)
        if p % 2 == 0:
            count_row[p // 2] = mm_nt(jnp.ones((8, edges), bf16), drawn) * (1.0 / edges)
        else:
            count_col[p // 2] = mm(drawn, jnp.ones((edges, LANES), bf16)) * (1.0 / edges)


def prep(slots, negs, edges, live, padded):
    total = slots.shape[1]
    batches = total // edges // 2
    return pl.pallas_call(
        prep_body,
        out_shape=[
            pltpu.HBM((total, padded), bf16),
            pltpu.HBM((live, total), bf16),
            pltpu.HBM((batches, 8, edges), f32),
            pltpu.HBM((batches, edges, LANES), f32),
        ],
        compiler_params=room(24),
        name="prep",
    )(slots, negs)


def lanes_of(shape):
    return lax.broadcasted_iota(jnp.int32, shape, 1)


def leftover(blocks):
    lane = lanes_of(blocks[0].shape)
    out = jnp.zeros(blocks[0].shape, f32)
    for c, block in enumerate(blocks):
        at = SPARE * c
        wide = SPARE if c < QUARTERS - 1 else 16
        moved = pltpu.roll(block, (at - (MAIN if c < QUARTERS - 1 else 0)) % LANES, 1)
        out = jnp.where((lane >= at) & (lane < at + wide), moved, out)
    return out


def grads_body(heads, tails, by_edge, by_slot, count_row, count_col, ahead, out_heads, out_tails,
               high, low, d_high, d_low, edge_part, slot_part, summed, packed, in_sems, out_sems):
    live = by_slot.shape[0]
    head_count = live - tails.shape[0]
    owners = head_count // 8
    tall = heads.shape[0] // owners
    padded = by_edge.shape[1]
    width = tails.shape[1]
    batches, _, edges = count_row.shape
    loads = []
    for p in range(2 * batches):
        span = pl.ds(p * edges, edges)
        loads.append(pltpu.make_async_copy(by_edge.at[span], edge_part.at[span], in_sems.at[p]))
        loads[-1].start()
    last = pltpu.make_async_copy(by_slot, slot_part, in_sems.at[2 * batches])
    last.start()
    ends = heads[pl.ds(tall - 1, owners, stride=tall), :]
    for k in range(8):
        span = slice(k * owners, (k + 1) * owners)
        for c in range(QUARTERS):
            lanes = slice(c * LANES, (c + 1) * LANES)
            if c < QUARTERS - 1:
                block = heads[pl.ds(8 * c + k, owners, stride=tall), :]
            else:
                block = pltpu.roll(ends, (LANES - 16 * k) % LANES, 1) if k else ends
                block = jnp.where(lanes_of(block.shape) < 16, block, 0.0)
            high[span, lanes], low[span, lanes] = halves(block)
    high[head_count:live, :], low[head_count:live, :] = halves(tails[...])
    high[live:, :] = jnp.zeros((padded - live, width), bf16)
    low[live:, :] = jnp.zeros((padded - live, width), bf16)

    def gathered(b):
        picks = []
        for side in range(2):
            at = (2 * b + side) * edges
            loads[2 * b + side].wait()
            chosen = edge_part[at : at + edges, :]
            picks.append((mm(chosen, high[...]).astype(bf16), mm(chosen, low[...]).astype(bf16)))
        return picks

    def scored(picks):
        (s_high, s_low), (t_high, t_low) = picks
        return mm_nt(s_high, t_high) + mm_nt(s_high, t_low) + mm_nt(s_low, t_high)

    def gained(b, scores):
        decay = jnp.exp2(jnp.minimum(scores * -LOG2E, 126.0))
        weight = 1.0 / (1.0 + decay)
        counts = count_row[b, 0:1, :] + jnp.concatenate([count_col[b]] * (edges // LANES), axis=1)
        gain = weight * counts
        eye = lanes_of((LANES, LANES)) == lax.broadcasted_iota(jnp.int32, (LANES, LANES), 0)
        bands = []
        for i in range(edges // LANES):
            span = slice(i * LANES, (i + 1) * LANES)
            missing = jnp.where(eye, decay[span, span] * weight[span, span], 0.0)
            row = [gain[span, : i * LANES], gain[span, span] - missing, gain[span, (i + 1) * LANES :]]
            bands.append(jnp.concatenate([part for part in row if part.shape[1]], axis=1))
        return jnp.concatenate(bands, axis=0)

    def pulled(at, g_high, g_low, high_rows, low_rows):
        moved = mm(g_high, high_rows) + mm(g_high, low_rows) + mm(g_low, high_rows)
        d_high[at : at + edges, :], d_low[at : at + edges, :] = halves(moved)

    picks = gathered(0)
    scores = scored(picks)
    for b in range(batches):
        if b + 1 < batches:
            next_picks = gathered(b + 1)
        gain = gained(b, scores)
        if b + 1 < batches:
            next_scores = scored(next_picks)
        g_high, g_low = halves(gain)
        pulled(2 * b * edges, g_high, g_low, *picks[1])
        pulled((2 * b + 1) * edges, g_high.T, g_low.T, *picks[0])
        if b + 1 < batches:
            picks, scores = next_picks, next_scores
    last.wait()
    stores = []
    block = 2 * LANES
    short = 7 * owners
    for h in range(width // block):
        span = slice(h * block, (h + 1) * block)
        summed[:, span] = mm(slot_part[...], d_high[:, span]) + mm(slot_part[...], d_low[:, span])
        for q in (2 * h, 2 * h + 1):

            def quarter(at, size):
                if q < QUARTERS - 1:
                    return summed[at : at + size, q * LANES : (q + 1) * LANES]
                return leftover([summed[at : at + size, c * LANES : (c + 1) * LANES] for c in range(QUARTERS)])

            eighth = quarter(7 * owners, owners)
            for k in range(7):
                value = quarter(k * owners, owners)
                if SPARE * k < MAIN:
                    moved = pltpu.roll(eighth, (MAIN - SPARE * k) % LANES, 1)
                    value = jnp.where(lanes_of(value.shape) < MAIN, value, moved)
                packed[pl.ds(q * short + k, owners, stride=7), :] = value
            out_tails[:, q * LANES : (q + 1) * LANES] = quarter(head_count, live - head_count)
        part = pl.ds(2 * h * short, 2 * short)
        stores.append(pltpu.make_async_copy(packed.at[part], out_heads.at[part], out_sems.at[h]))
        stores[-1].start()
    for store in stores:
        store.wait()


def grads(heads, tails, by_edge, by_slot, count_row, count_col, ahead):
    width = tails.shape[1]
    total, padded = by_edge.shape
    live = by_slot.shape[0]
    shape = (QUARTERS * 7 * (live - tails.shape[0]) // 8, LANES)
    return pl.pallas_call(
        grads_body,
        in_specs=[VMEM, VMEM, HBM, HBM, VMEM, VMEM, HBM],
        out_specs=[HBM, VMEM],
        out_shape=[pltpu.HBM(shape, f32), jax.ShapeDtypeStruct(tails.shape, f32)],
        scratch_shapes=[
            pltpu.VMEM((padded, width), bf16),
            pltpu.VMEM((padded, width), bf16),
            pltpu.VMEM((total, width), bf16),
            pltpu.VMEM((total, width), bf16),
            pltpu.VMEM(by_edge.shape, bf16),
            pltpu.VMEM(by_slot.shape, bf16),
            pltpu.VMEM((live, width), f32),
            pltpu.VMEM(shape, f32),
            pltpu.SemaphoreType.DMA((2 * count_row.shape[0] + 1,)),
            pltpu.SemaphoreType.DMA((width // LANES // 2,)),
        ],
        compiler_params=room(48),
        name="grads",
    )(near(heads), tails, far(by_edge), far(by_slot), count_row, count_col, far(ahead))


def hot_body(me, *refs):
    lists, hot = refs[:-1], refs[-1]
    rows = hot.shape[0]
    groups = len(lists)
    tail_count = HEAVY * 8
    head_count = lists[0].shape[1] - tail_count
    for s, ids in enumerate(lists):
        group = (me[0] + s) % groups
        down = lax.broadcasted_iota(jnp.int32, (rows, head_count), 0)
        spot = pl.multiple_of(group * head_count, LANES)
        hot[:, pl.ds(spot, head_count)] = jnp.where(down == ids[:, :head_count], 1.0, 0.0).astype(bf16)
    tails = jnp.concatenate([ids[:, head_count:] for ids in lists], axis=1)
    down = lax.broadcasted_iota(jnp.int32, (rows, tails.shape[1]), 0)
    hot[:, groups * head_count :] = jnp.where(down == tails, 1.0, 0.0).astype(bf16)


def hot_rows(me, lists, rows):
    vmem = pl.BlockSpec(memory_space=pltpu.VMEM)
    return pl.pallas_call(
        hot_body,
        in_specs=[pl.BlockSpec(memory_space=pltpu.SMEM)] + [vmem] * len(lists),
        out_shape=pltpu.HBM((rows, len(lists) * lists[0].shape[1]), bf16),
        compiler_params=room(16),
        name="hot",
    )(me, *lists)


def owner_body(back, tails, hot, out, spots, sems):
    parts = sems.shape[0] - 1
    short = back.shape[0] // parts
    each = short // 7 * 8
    owners = short // 7
    spans = [(p * each, each) for p in range(parts)] + [(parts * each, tails.shape[0])]
    loads = []
    for p, (at, size) in enumerate(spans):
        loads.append(pltpu.make_async_copy(hot.at[:, pl.ds(at, size)], spots.at[:, pl.ds(at, size)], sems.at[p]))
        loads[-1].start()
    total = None
    for p, (at, size) in enumerate(spans):
        if p < parts:
            eighth = jnp.zeros((owners, LANES), f32)
            lane = lanes_of(eighth.shape)
            for k in range(-(-MAIN // SPARE)):
                moved = pltpu.roll(back[pl.ds(p * short + k, owners, stride=7), :], (SPARE * k - MAIN) % LANES, 1)
                eighth = jnp.where((lane >= SPARE * k) & (lane < SPARE * (k + 1)), moved, eighth)
            values = jnp.concatenate([back[p * short : (p + 1) * short, :], eighth], axis=0)
        else:
            values = tails[...]
        both = jnp.concatenate(halves(values), axis=1)
        loads[p].wait()
        part = mm(spots[:, at : at + size], both)
        total = part if total is None else total + part
    summed = total[:, :LANES] + total[:, LANES:]
    out[...] = summed.T[: out.shape[0], :]


def owner(back, tails, hot):
    return pl.pallas_call(
        owner_body,
        in_specs=[VMEM, VMEM, HBM],
        out_specs=VMEM,
        out_shape=jax.ShapeDtypeStruct((MAIN, hot.shape[0]), f32),
        scratch_shapes=[pltpu.VMEM(hot.shape, bf16), pltpu.SemaphoreType.DMA((5,))],
        compiler_params=room(16),
        name="owner",
    )(near(back), tails, far(hot))


def update_body(me, own, next1, next2, next3, rows, sums, new_rows, new_sums, quarters, fresh_rows, sems):
    for s, piece in enumerate((own, next1, next2, next3)):
        quarters[(me[0] + 4 - s) % 4] = piece[...]
    squares = jnp.zeros(sums.shape, f32)
    for q in range(QUARTERS):
        squares += jnp.sum(quarters[q] * quarters[q], axis=0, keepdims=True)
    fresh = sums[...] + squares * (1.0 / rows.shape[0])
    new_sums[...] = fresh
    scale = LEARN_RATE / jnp.sqrt(fresh)
    depth = rows.shape[0]
    stores = []
    for c in range(QUARTERS - 1):
        at = c * LANES
        end = at + LANES
        wide = SPARE
        if c == QUARTERS - 2:
            end = depth
            wide = depth - at - MAIN
        main = slice(at, at + MAIN)
        rest = slice(at + MAIN, end)
        fresh_rows[main, :] = rows[main, :] - quarters[c] * scale
        fresh_rows[rest, :] = rows[rest, :] - quarters[QUARTERS - 1, SPARE * c : SPARE * c + wide, :] * scale
        span = pl.ds(at, end - at)
        stores.append(pltpu.make_async_copy(fresh_rows.at[span], new_rows.at[span], sems.at[c]))
        stores[-1].start()
    for store in stores:
        store.wait()


def update(me, pieces, rows, sums):
    return pl.pallas_call(
        update_body,
        in_specs=[SMEM] + [VMEM] * len(pieces) + [VMEM, VMEM],
        out_specs=[HBM, VMEM],
        out_shape=[
            jax.ShapeDtypeStruct(rows.shape, f32),
            jax.ShapeDtypeStruct(sums.shape, f32),
        ],
        scratch_shapes=[
            pltpu.VMEM((len(pieces), *pieces[0].shape), f32),
            pltpu.VMEM(rows.shape, f32),
            pltpu.SemaphoreType.DMA((len(pieces),)),
        ],
        compiler_params=room(16),
        name="update",
    )(me, *[near(piece) for piece in pieces], near(rows), sums)


def compact(slots, here, owners, capacity):
    half = capacity // 2
    who, k = slots // capacity, slots % capacity
    return jnp.where(k < half, k * owners + who, owners * half + (who - here) % owners * half + k - half)


def local(embedding, adagrad_sum, row_lists, source_slots, target_slots, negative_ids):
    requests = row_lists[0, 0]
    owners, capacity = requests.shape
    half = capacity // 2
    rows = embedding.shape[0]
    groups = lax.axis_size("rep")
    edges = source_slots.shape[3]
    here = lax.axis_index("dom")
    given = exchanged(requests.reshape(owners, 1, capacity), "dom")
    incoming = given.reshape(owners, capacity)
    columns = embedding.T
    spread = spread_rows(columns)
    slots = jnp.stack([source_slots[0, 0], target_slots[0, 0]], axis=1).reshape(1, -1)
    slots = compact(slots, here, owners, capacity)
    live = owners * half + HEAVY * half
    padded = -(-live // LANES) * LANES
    plan = prep(slots, negative_ids[0, 0].reshape(1, -1), edges, live, padded)

    heads, tails = serve(given, here.reshape(1).astype(jnp.int32), spread)
    tails = tails.reshape(HEAVY, half, -1)
    tails = jnp.concatenate(
        [tails[0]] + [passed_along(tails[r], "dom", -r) for r in range(1, HEAVY)], axis=0
    )
    heads = exchanged(heads.reshape(owners, -1, 1, LANES), "dom").reshape(-1, LANES)
    me = lax.axis_index("rep")
    mine = me.reshape(1).astype(jnp.int32)
    askers = jnp.arange(owners)[None, :] == ((here - jnp.arange(HEAVY)) % owners)[:, None]
    tail_ids = jnp.sum(jnp.where(askers[:, :, None], incoming[None, :, half:], 0), axis=1)
    ids = [incoming[:, : half - 1], incoming[:, half - 1], tail_ids]
    ids = jnp.concatenate([part.reshape(1, -1) for part in ids], axis=1)
    listed = [ids] + [passed_along(ids, "rep", -s) for s in range(1, groups)]
    hot = hot_rows(mine, listed, rows)

    head_grads, tail_grads = grads(heads, tails, *plan, hot)
    back = exchanged(head_grads.reshape(groups * owners, half - 1, 1, LANES), ("rep", "dom"))
    tail_grads = jnp.moveaxis(tail_grads.reshape(HEAVY * half, groups, LANES), 1, 0)
    wanted = [
        lax.dynamic_index_in_dim(tail_grads, (me + groups - s) % groups, 0, keepdims=False)
        for s in range(groups)
    ]
    tail_grads = jnp.stack(
        [wanted[0]] + [passed_along(wanted[s], "rep", -s) for s in range(1, groups)], axis=0
    ).reshape(groups, HEAVY, half, LANES)
    tail_back = [tail_grads[:, 0]] + [passed_along(tail_grads[:, r], "dom", r) for r in range(1, HEAVY)]
    tail_back = jnp.stack(tail_back, axis=1).reshape(-1, LANES)
    quarter = owner(back.reshape(-1, LANES), tail_back, hot)
    pieces = [quarter] + [passed_along(quarter, "rep", s) for s in range(1, groups)]
    new_rows, new_sums = update(mine, pieces, columns, adagrad_sum.reshape(1, -1))
    return new_rows.T, new_sums.reshape(-1)


def solution(mesh):
    in_specs = (
        P("dom", None),
        P("dom"),
        P("rep", "dom", None, None),
        P("rep", "dom", None, None),
        P("rep", "dom", None, None),
        P("rep", "dom", None, None, None),
    )
    out_specs = (P("dom", None), P("dom"))

    return jax.shard_map(local, mesh=mesh, in_specs=in_specs, out_specs=out_specs, check_vma=False)
```

```python
import jax
import jax.numpy as jnp
from jax import lax
from jax.experimental import pallas as pl
from jax.experimental.pallas import tpu as pltpu
from jax.sharding import PartitionSpec as P


HEAVY = 4
LEARN_RATE = 0.1
LOG2E = 1.4426950408889634
LANES = 128
MAIN = 104
SPARE = LANES - MAIN
QUARTERS = 4
f32 = jnp.float32
bf16 = jnp.bfloat16


def passed_along(value, axis, steps):
    count = lax.axis_size(axis)
    pairs = [(source, (source + steps) % count) for source in range(count)]
    return lax.ppermute(value, axis, pairs)


def exchanged(value, axis):
    return lax.all_to_all(value, axis, 0, 0, tiled=True)


def halves(x):
    high = x.astype(bf16)
    low = (x - high.astype(f32)).astype(bf16)
    return high, low


VMEM = pl.BlockSpec(memory_space=pltpu.VMEM)
SMEM = pl.BlockSpec(memory_space=pltpu.SMEM)
HBM = pl.BlockSpec(memory_space=pltpu.HBM)


def room(mib):
    return pltpu.CompilerParams(vmem_limit_bytes=mib << 20)


def far(x):
    return pltpu.with_memory_space_constraint(x, pltpu.HBM)


def near(x):
    return pltpu.with_memory_space_constraint(x, pltpu.VMEM)


def mm(a, b):
    return jnp.dot(a, b, preferred_element_type=f32)


def mm_nt(a, b):
    return lax.dot_general(a, b, (((1,), (1,)), ((), ())), preferred_element_type=f32)


def spread_body(columns, out):
    depth, rows = columns.shape
    for c in range(out.shape[1]):
        piece = columns[c * LANES : min((c + 1) * LANES, depth), :]
        if piece.shape[0] < LANES:
            piece = jnp.concatenate([piece, jnp.zeros((LANES - piece.shape[0], rows), f32)], axis=0)
        out[:, c, :] = piece.T


def spread_rows(columns):
    return pl.pallas_call(
        spread_body,
        out_specs=VMEM,
        out_shape=pltpu.VMEM((columns.shape[1], QUARTERS, LANES), f32),
        compiler_params=room(16),
        name="spread",
    )(columns)


def serve_body(ids, here, rows, heads, tails, picked, ends, sems):
    owners = ids.shape[0]
    parts = sems.shape[0]
    each = owners // parts
    blocks = QUARTERS - 1
    tall = 8 * blocks + 1

    def eight(w, carry):
        taken = [rows[ids[w, 0, k]] for k in range(8)]
        for k in range(8):
            picked[pl.ds(w * tall + k, blocks, stride=8), :] = taken[k][:blocks]
            ends[pl.ds(w * 8 + k, 1), :] = taken[k][blocks:]
        return carry

    for reach in range(HEAVY):
        asker = (here[0] + owners - reach) % owners
        for k in range(8):
            row = rows[ids[asker, 0, 8 + k]]
            for c in range(QUARTERS):
                tails[reach * 8 + k : reach * 8 + k + 1, c * LANES : (c + 1) * LANES] = row[c : c + 1]
    copies = []
    for part in range(parts):
        lax.fori_loop(part * each, (part + 1) * each, eight, 0, unroll=4)
        joined = ends[pl.ds(part * each * 8, each, stride=8), :]
        for k in range(1, 8):
            joined += pltpu.roll(ends[pl.ds(part * each * 8 + k, each, stride=8), :], 16 * k, 1)
        picked[pl.ds(part * each * tall + tall - 1, each, stride=tall), :] = joined
        span = pl.ds(part * each * tall, each * tall)
        copies.append(pltpu.make_async_copy(picked.at[span], heads.at[span], sems.at[part]))
        copies[-1].start()
    for copy in copies:
        copy.wait()


def serve(ids, here, rows):
    width = QUARTERS * LANES
    owners = ids.shape[0]
    shape = (owners * (8 * (QUARTERS - 1) + 1), LANES)
    return pl.pallas_call(
        serve_body,
        in_specs=[SMEM, SMEM, VMEM],
        out_specs=[HBM, VMEM],
        out_shape=[pltpu.HBM(shape, f32), jax.ShapeDtypeStruct((HEAVY * 8, width), f32)],
        scratch_shapes=[
            pltpu.VMEM(shape, f32),
            pltpu.VMEM((owners * 8, LANES), f32),
            pltpu.SemaphoreType.DMA((4,)),
        ],
        compiler_params=room(16),
        name="serve",
    )(ids, here, near(rows))


def prep_body(slots, negs, by_edge, by_slot, count_row, count_col):
    edges = count_row.shape[2]
    parts = slots.shape[1] // edges
    live = by_slot.shape[0]
    padded = by_edge.shape[1]
    one, zero = jnp.ones((), f32), jnp.zeros((), f32)
    for p in range(parts):
        row = slots[:, p * edges : (p + 1) * edges]
        down = lax.broadcasted_iota(jnp.int32, (live, edges), 0)
        by_slot[:, p * edges : (p + 1) * edges] = jnp.where(down == row, one, zero).astype(bf16)
        column = jnp.broadcast_to(row, (LANES, edges)).T
        across = lax.broadcasted_iota(jnp.int32, (edges, LANES), 1)
        blocks = padded // LANES
        for c in range(blocks):
            hit = across + c * LANES == column
            if c == blocks - 1:
                count = HEAVY * 8
                hit = hit | ((across >= count) & (across + (c * LANES - count) == column))
            by_edge[p * edges : (p + 1) * edges, c * LANES : (c + 1) * LANES] = jnp.where(hit, one, zero).astype(bf16)
        neg = negs[:, p * edges : (p + 1) * edges]
        down = lax.broadcasted_iota(jnp.int32, (edges, edges), 0)
        drawn = jnp.where(down == neg, one, zero).astype(bf16)
        if p % 2 == 0:
            count_row[p // 2] = mm_nt(jnp.ones((8, edges), bf16), drawn) * (1.0 / edges)
        else:
            count_col[p // 2] = mm(drawn, jnp.ones((edges, LANES), bf16)) * (1.0 / edges)


def prep(slots, negs, edges, live, padded):
    total = slots.shape[1]
    batches = total // edges // 2
    return pl.pallas_call(
        prep_body,
        out_shape=[
            pltpu.HBM((total, padded), bf16),
            pltpu.HBM((live, total), bf16),
            pltpu.HBM((batches, 8, edges), f32),
            pltpu.HBM((batches, edges, LANES), f32),
        ],
        compiler_params=room(24),
        name="prep",
    )(slots, negs)


def lanes_of(shape):
    return lax.broadcasted_iota(jnp.int32, shape, 1)


def leftover(blocks):
    lane = lanes_of(blocks[0].shape)
    out = jnp.zeros(blocks[0].shape, f32)
    for c, block in enumerate(blocks):
        at = SPARE * c
        wide = SPARE if c < QUARTERS - 1 else 16
        moved = pltpu.roll(block, (at - (MAIN if c < QUARTERS - 1 else 0)) % LANES, 1)
        out = jnp.where((lane >= at) & (lane < at + wide), moved, out)
    return out


def grads_body(heads, tails, by_edge, by_slot, count_row, count_col, ahead, out_heads, out_tails,
               high, low, extra, d_high, d_low, edge_part, slot_part, summed, packed, in_sems, out_sems):
    live = by_slot.shape[0]
    head_count = live - tails.shape[0]
    owners = head_count // 8
    tall = heads.shape[0] // owners
    padded = by_edge.shape[1]
    width = tails.shape[1]
    batches, _, edges = count_row.shape
    loads = []
    for p in range(2 * batches):
        span = pl.ds(p * edges, edges)
        loads.append(pltpu.make_async_copy(by_edge.at[span], edge_part.at[span], in_sems.at[p]))
        loads[-1].start()
    last = pltpu.make_async_copy(by_slot, slot_part, in_sems.at[2 * batches])
    last.start()
    ends = heads[pl.ds(tall - 1, owners, stride=tall), :]
    for k in range(8):
        span = slice(k * owners, (k + 1) * owners)
        for c in range(QUARTERS):
            lanes = slice(c * LANES, (c + 1) * LANES)
            if c < QUARTERS - 1:
                block = heads[pl.ds(8 * c + k, owners, stride=tall), :]
            else:
                block = pltpu.roll(ends, (LANES - 16 * k) % LANES, 1) if k else ends
                block = jnp.where(lanes_of(block.shape) < 16, block, 0.0)
            high[span, lanes], low[span, lanes] = halves(block)
    pieces = list(halves(tails[...]))
    pieces.append(jnp.zeros((padded - head_count - 2 * tails.shape[0], width), bf16))
    extra[...] = jnp.concatenate(pieces, axis=0)

    def gathered(b):
        picks = []
        for side in range(2):
            at = (2 * b + side) * edges
            loads[2 * b + side].wait()
            chosen = edge_part[at : at + edges, :head_count]
            rest = edge_part[at : at + edges, head_count:]
            picks.append(mm(chosen, high[...]) + mm(chosen, low[...]) + mm(rest, extra[...]))
        return picks

    def gained(b, scores):
        decay = jnp.exp2(jnp.minimum(scores * -LOG2E, 126.0))
        weight = 1.0 / (1.0 + decay)
        counts = count_row[b, 0:1, :] + jnp.concatenate([count_col[b]] * (edges // LANES), axis=1)
        return (weight * counts).astype(bf16)

    def pulled(at, gain, pull, rows_high, rows_low, rows):
        moved = mm(gain, rows_high) + mm(gain, rows_low) + pull * rows
        d_high[at : at + edges, :], d_low[at : at + edges, :] = halves(moved)

    for b in range(batches):
        s_rows, t_rows = gathered(b)
        s_high, s_low = halves(s_rows)
        t_high, t_low = halves(t_rows)
        positive = jnp.sum(s_rows * t_rows, axis=1, keepdims=True)
        falling = jnp.exp(-jnp.abs(positive))
        pull = -jnp.where(positive >= 0, falling, 1.0) / (1.0 + falling)
        gain = gained(b, mm_nt(s_high, t_high))
        pulled(2 * b * edges, gain, pull, t_high, t_low, t_rows)
        pulled((2 * b + 1) * edges, gain.T, pull, s_high, s_low, s_rows)
    last.wait()
    stores = []
    block = 2 * LANES
    short = 7 * owners
    for h in range(width // block):
        span = slice(h * block, (h + 1) * block)
        summed[:, span] = mm(slot_part[...], d_high[:, span]) + mm(slot_part[...], d_low[:, span])
        for q in (2 * h, 2 * h + 1):

            def quarter(at, size):
                if q < QUARTERS - 1:
                    return summed[at : at + size, q * LANES : (q + 1) * LANES]
                return leftover([summed[at : at + size, c * LANES : (c + 1) * LANES] for c in range(QUARTERS)])

            eighth = quarter(7 * owners, owners)
            for k in range(7):
                value = quarter(k * owners, owners)
                if SPARE * k < MAIN:
                    moved = pltpu.roll(eighth, (MAIN - SPARE * k) % LANES, 1)
                    value = jnp.where(lanes_of(value.shape) < MAIN, value, moved)
                packed[pl.ds(q * short + k, owners, stride=7), :] = value
            out_tails[:, q * LANES : (q + 1) * LANES] = quarter(head_count, live - head_count)
        part = pl.ds(2 * h * short, 2 * short)
        stores.append(pltpu.make_async_copy(packed.at[part], out_heads.at[part], out_sems.at[h]))
        stores[-1].start()
    for store in stores:
        store.wait()


def grads(heads, tails, by_edge, by_slot, count_row, count_col, ahead):
    width = tails.shape[1]
    total, padded = by_edge.shape
    live = by_slot.shape[0]
    shape = (QUARTERS * 7 * (live - tails.shape[0]) // 8, LANES)
    return pl.pallas_call(
        grads_body,
        in_specs=[VMEM, VMEM, HBM, HBM, VMEM, VMEM, HBM],
        out_specs=[HBM, VMEM],
        out_shape=[pltpu.HBM(shape, f32), jax.ShapeDtypeStruct(tails.shape, f32)],
        scratch_shapes=[
            pltpu.VMEM((live - tails.shape[0], width), bf16),
            pltpu.VMEM((live - tails.shape[0], width), bf16),
            pltpu.VMEM((padded - live + tails.shape[0], width), bf16),
            pltpu.VMEM((total, width), bf16),
            pltpu.VMEM((total, width), bf16),
            pltpu.VMEM(by_edge.shape, bf16),
            pltpu.VMEM(by_slot.shape, bf16),
            pltpu.VMEM((live, width), f32),
            pltpu.VMEM(shape, f32),
            pltpu.SemaphoreType.DMA((2 * count_row.shape[0] + 1,)),
            pltpu.SemaphoreType.DMA((width // LANES // 2,)),
        ],
        compiler_params=room(48),
        name="grads",
    )(near(heads), tails, far(by_edge), far(by_slot), count_row, count_col, far(ahead))


def hot_body(me, *refs):
    lists, hot = refs[:-1], refs[-1]
    rows = hot.shape[0]
    groups = len(lists)
    tail_count = HEAVY * 8
    head_count = lists[0].shape[1] - tail_count
    for s, ids in enumerate(lists):
        group = (me[0] + s) % groups
        down = lax.broadcasted_iota(jnp.int32, (rows, head_count), 0)
        spot = pl.multiple_of(group * head_count, LANES)
        hot[:, pl.ds(spot, head_count)] = jnp.where(down == ids[:, :head_count], 1.0, 0.0).astype(bf16)
    tails = jnp.concatenate([ids[:, head_count:] for ids in lists], axis=1)
    down = lax.broadcasted_iota(jnp.int32, (rows, tails.shape[1]), 0)
    hot[:, groups * head_count :] = jnp.where(down == tails, 1.0, 0.0).astype(bf16)


def hot_rows(me, lists, rows):
    vmem = pl.BlockSpec(memory_space=pltpu.VMEM)
    return pl.pallas_call(
        hot_body,
        in_specs=[pl.BlockSpec(memory_space=pltpu.SMEM)] + [vmem] * len(lists),
        out_shape=pltpu.HBM((rows, len(lists) * lists[0].shape[1]), bf16),
        compiler_params=room(16),
        name="hot",
    )(me, *lists)


def owner_body(back, tails, hot, out, spots, sems):
    parts = sems.shape[0] - 1
    short = back.shape[0] // parts
    each = short // 7 * 8
    owners = short // 7
    spans = [(p * each, each) for p in range(parts)] + [(parts * each, tails.shape[0])]
    loads = []
    for p, (at, size) in enumerate(spans):
        loads.append(pltpu.make_async_copy(hot.at[:, pl.ds(at, size)], spots.at[:, pl.ds(at, size)], sems.at[p]))
        loads[-1].start()
    total = None
    for p, (at, size) in enumerate(spans):
        if p < parts:
            eighth = jnp.zeros((owners, LANES), f32)
            lane = lanes_of(eighth.shape)
            for k in range(-(-MAIN // SPARE)):
                moved = pltpu.roll(back[pl.ds(p * short + k, owners, stride=7), :], (SPARE * k - MAIN) % LANES, 1)
                eighth = jnp.where((lane >= SPARE * k) & (lane < SPARE * (k + 1)), moved, eighth)
            values = jnp.concatenate([back[p * short : (p + 1) * short, :], eighth], axis=0)
        else:
            values = tails[...]
        both = jnp.concatenate(halves(values), axis=1)
        loads[p].wait()
        part = mm(spots[:, at : at + size], both)
        total = part if total is None else total + part
    summed = total[:, :LANES] + total[:, LANES:]
    out[...] = summed.T[: out.shape[0], :]


def owner(back, tails, hot):
    return pl.pallas_call(
        owner_body,
        in_specs=[VMEM, VMEM, HBM],
        out_specs=VMEM,
        out_shape=jax.ShapeDtypeStruct((MAIN, hot.shape[0]), f32),
        scratch_shapes=[pltpu.VMEM(hot.shape, bf16), pltpu.SemaphoreType.DMA((5,))],
        compiler_params=room(16),
        name="owner",
    )(near(back), tails, far(hot))


def update_body(me, own, next1, next2, next3, rows, sums, new_rows, new_sums, quarters, fresh_rows, sems):
    for s, piece in enumerate((own, next1, next2, next3)):
        quarters[(me[0] + 4 - s) % 4] = piece[...]
    squares = jnp.zeros(sums.shape, f32)
    for q in range(QUARTERS):
        squares += jnp.sum(quarters[q] * quarters[q], axis=0, keepdims=True)
    fresh = sums[...] + squares * (1.0 / rows.shape[0])
    new_sums[...] = fresh
    scale = LEARN_RATE / jnp.sqrt(fresh)
    depth = rows.shape[0]
    stores = []
    for c in range(QUARTERS - 1):
        at = c * LANES
        end = at + LANES
        wide = SPARE
        if c == QUARTERS - 2:
            end = depth
            wide = depth - at - MAIN
        main = slice(at, at + MAIN)
        rest = slice(at + MAIN, end)
        fresh_rows[main, :] = rows[main, :] - quarters[c] * scale
        fresh_rows[rest, :] = rows[rest, :] - quarters[QUARTERS - 1, SPARE * c : SPARE * c + wide, :] * scale
        span = pl.ds(at, end - at)
        stores.append(pltpu.make_async_copy(fresh_rows.at[span], new_rows.at[span], sems.at[c]))
        stores[-1].start()
    for store in stores:
        store.wait()


def update(me, pieces, rows, sums):
    return pl.pallas_call(
        update_body,
        in_specs=[SMEM] + [VMEM] * len(pieces) + [VMEM, VMEM],
        out_specs=[HBM, VMEM],
        out_shape=[
            jax.ShapeDtypeStruct(rows.shape, f32),
            jax.ShapeDtypeStruct(sums.shape, f32),
        ],
        scratch_shapes=[
            pltpu.VMEM((len(pieces), *pieces[0].shape), f32),
            pltpu.VMEM(rows.shape, f32),
            pltpu.SemaphoreType.DMA((len(pieces),)),
        ],
        compiler_params=room(16),
        name="update",
    )(me, *[near(piece) for piece in pieces], near(rows), sums)


def compact(slots, here, owners, capacity):
    half = capacity // 2
    who, k = slots // capacity, slots % capacity
    return jnp.where(k < half, k * owners + who, owners * half + (who - here) % owners * half + k - half)


def local(embedding, adagrad_sum, row_lists, source_slots, target_slots, negative_ids):
    requests = row_lists[0, 0]
    owners, capacity = requests.shape
    half = capacity // 2
    rows = embedding.shape[0]
    groups = lax.axis_size("rep")
    edges = source_slots.shape[3]
    here = lax.axis_index("dom")
    given = exchanged(requests.reshape(owners, 1, capacity), "dom")
    incoming = given.reshape(owners, capacity)
    columns = embedding.T
    spread = spread_rows(columns)
    slots = jnp.stack([source_slots[0, 0], target_slots[0, 0]], axis=1).reshape(1, -1)
    slots = compact(slots, here, owners, capacity)
    live = owners * half + HEAVY * half
    padded = -(-live // LANES) * LANES
    plan = prep(slots, negative_ids[0, 0].reshape(1, -1), edges, live, padded)

    heads, tails = serve(given, here.reshape(1).astype(jnp.int32), spread)
    tails = tails.reshape(HEAVY, half, -1)
    tails = jnp.concatenate(
        [tails[0]] + [passed_along(tails[r], "dom", -r) for r in range(1, HEAVY)], axis=0
    )
    heads = exchanged(heads.reshape(owners, -1, 1, LANES), "dom").reshape(-1, LANES)
    me = lax.axis_index("rep")
    mine = me.reshape(1).astype(jnp.int32)
    askers = jnp.arange(owners)[None, :] == ((here - jnp.arange(HEAVY)) % owners)[:, None]
    tail_ids = jnp.sum(jnp.where(askers[:, :, None], incoming[None, :, half:], 0), axis=1)
    ids = [incoming[:, : half - 1], incoming[:, half - 1], tail_ids]
    ids = jnp.concatenate([part.reshape(1, -1) for part in ids], axis=1)
    listed = [ids] + [passed_along(ids, "rep", -s) for s in range(1, groups)]
    hot = hot_rows(mine, listed, rows)

    head_grads, tail_grads = grads(heads, tails, *plan, hot)
    back = exchanged(head_grads.reshape(groups * owners, half - 1, 1, LANES), ("rep", "dom"))
    tail_grads = jnp.moveaxis(tail_grads.reshape(HEAVY * half, groups, LANES), 1, 0)
    wanted = [
        lax.dynamic_index_in_dim(tail_grads, (me + groups - s) % groups, 0, keepdims=False)
        for s in range(groups)
    ]
    tail_grads = jnp.stack(
        [wanted[0]] + [passed_along(wanted[s], "rep", -s) for s in range(1, groups)], axis=0
    ).reshape(groups, HEAVY, half, LANES)
    tail_back = [tail_grads[:, 0]] + [passed_along(tail_grads[:, r], "dom", r) for r in range(1, HEAVY)]
    tail_back = jnp.stack(tail_back, axis=1).reshape(-1, LANES)
    quarter = owner(back.reshape(-1, LANES), tail_back, hot)
    pieces = [quarter] + [passed_along(quarter, "rep", s) for s in range(1, groups)]
    new_rows, new_sums = update(mine, pieces, columns, adagrad_sum.reshape(1, -1))
    return new_rows.T, new_sums.reshape(-1)


def solution(mesh):
    in_specs = (
        P("dom", None),
        P("dom"),
        P("rep", "dom", None, None),
        P("rep", "dom", None, None),
        P("rep", "dom", None, None),
        P("rep", "dom", None, None, None),
    )
    out_specs = (P("dom", None), P("dom"))

    return jax.shard_map(local, mesh=mesh, in_specs=in_specs, out_specs=out_specs, check_vma=False)
```

```python
import jax
import jax.numpy as jnp
from jax import lax
from jax.experimental import pallas as pl
from jax.experimental.pallas import tpu as pltpu
from jax.sharding import PartitionSpec as P


HEAVY = 4
LEARN_RATE = 0.1
LOG2E = 1.4426950408889634
LANES = 128
MAIN = 104
SPARE = LANES - MAIN
QUARTERS = 4
f32 = jnp.float32
bf16 = jnp.bfloat16


def passed_along(value, axis, steps):
    count = lax.axis_size(axis)
    pairs = [(source, (source + steps) % count) for source in range(count)]
    return lax.ppermute(value, axis, pairs)


def exchanged(value, axis):
    return lax.all_to_all(value, axis, 0, 0, tiled=True)


def halves(x):
    high = x.astype(bf16)
    low = (x - high.astype(f32)).astype(bf16)
    return high, low


VMEM = pl.BlockSpec(memory_space=pltpu.VMEM)
SMEM = pl.BlockSpec(memory_space=pltpu.SMEM)
HBM = pl.BlockSpec(memory_space=pltpu.HBM)


def room(mib):
    return pltpu.CompilerParams(vmem_limit_bytes=mib << 20)


def far(x):
    return pltpu.with_memory_space_constraint(x, pltpu.HBM)


def near(x):
    return pltpu.with_memory_space_constraint(x, pltpu.VMEM)


def mm(a, b):
    return jnp.dot(a, b, preferred_element_type=f32)


def mm_nt(a, b):
    return lax.dot_general(a, b, (((1,), (1,)), ((), ())), preferred_element_type=f32)


def spread_body(columns, out):
    depth, rows = columns.shape
    for c in range(out.shape[1]):
        piece = columns[c * LANES : min((c + 1) * LANES, depth), :]
        if piece.shape[0] < LANES:
            piece = jnp.concatenate([piece, jnp.zeros((LANES - piece.shape[0], rows), f32)], axis=0)
        out[:, c, :] = piece.T


def spread_rows(columns):
    return pl.pallas_call(
        spread_body,
        out_specs=VMEM,
        out_shape=pltpu.VMEM((columns.shape[1], QUARTERS, LANES), f32),
        compiler_params=room(16),
        name="spread",
    )(columns)


def serve_body(ids, here, rows, heads, tails, picked, ends, sems):
    owners = ids.shape[0]
    parts = sems.shape[0]
    each = owners // parts
    blocks = QUARTERS - 1
    tall = 8 * blocks + 1

    def eight(w, carry):
        taken = [rows[ids[w, 0, k]] for k in range(8)]
        for k in range(8):
            picked[pl.ds(w * tall + k, blocks, stride=8), :] = taken[k][:blocks]
            ends[pl.ds(w * 8 + k, 1), :] = taken[k][blocks:]
        return carry

    for reach in range(HEAVY):
        asker = (here[0] + owners - reach) % owners
        for k in range(8):
            row = rows[ids[asker, 0, 8 + k]]
            for c in range(QUARTERS):
                tails[reach * 8 + k : reach * 8 + k + 1, c * LANES : (c + 1) * LANES] = row[c : c + 1]
    copies = []
    for part in range(parts):
        lax.fori_loop(part * each, (part + 1) * each, eight, 0, unroll=4)
        joined = ends[pl.ds(part * each * 8, each, stride=8), :]
        for k in range(1, 8):
            joined += pltpu.roll(ends[pl.ds(part * each * 8 + k, each, stride=8), :], 16 * k, 1)
        picked[pl.ds(part * each * tall + tall - 1, each, stride=tall), :] = joined
        span = pl.ds(part * each * tall, each * tall)
        copies.append(pltpu.make_async_copy(picked.at[span], heads.at[span], sems.at[part]))
        copies[-1].start()
    for copy in copies:
        copy.wait()


def serve(ids, here, rows):
    width = QUARTERS * LANES
    owners = ids.shape[0]
    shape = (owners * (8 * (QUARTERS - 1) + 1), LANES)
    return pl.pallas_call(
        serve_body,
        in_specs=[SMEM, SMEM, VMEM],
        out_specs=[HBM, VMEM],
        out_shape=[pltpu.HBM(shape, f32), jax.ShapeDtypeStruct((HEAVY * 8, width), f32)],
        scratch_shapes=[
            pltpu.VMEM(shape, f32),
            pltpu.VMEM((owners * 8, LANES), f32),
            pltpu.SemaphoreType.DMA((4,)),
        ],
        compiler_params=room(16),
        name="serve",
    )(ids, here, near(rows))


def prep_body(slots, negs, by_edge, by_slot, count_row, count_col):
    edges = count_row.shape[2]
    parts = slots.shape[1] // edges
    live = by_slot.shape[0]
    padded = by_edge.shape[1]
    one, zero = jnp.ones((), f32), jnp.zeros((), f32)
    for p in range(parts):
        row = slots[:, p * edges : (p + 1) * edges]
        down = lax.broadcasted_iota(jnp.int32, (live, edges), 0)
        by_slot[:, p * edges : (p + 1) * edges] = jnp.where(down == row, one, zero).astype(bf16)
        column = jnp.broadcast_to(row, (LANES, edges)).T
        across = lax.broadcasted_iota(jnp.int32, (edges, LANES), 1)
        blocks = padded // LANES
        for c in range(blocks):
            hit = across + c * LANES == column
            if c == blocks - 1:
                count = HEAVY * 8
                hit = hit | ((across >= count) & (across + (c * LANES - count) == column))
            by_edge[p * edges : (p + 1) * edges, c * LANES : (c + 1) * LANES] = jnp.where(hit, one, zero).astype(bf16)
        neg = negs[:, p * edges : (p + 1) * edges]
        down = lax.broadcasted_iota(jnp.int32, (edges, edges), 0)
        drawn = jnp.where(down == neg, one, zero).astype(bf16)
        if p % 2 == 0:
            count_row[p // 2] = mm_nt(jnp.ones((8, edges), bf16), drawn) * (1.0 / edges)
        else:
            count_col[p // 2] = mm(drawn, jnp.ones((edges, LANES), bf16)) * (1.0 / edges)


def prep(slots, negs, edges, live, padded):
    total = slots.shape[1]
    batches = total // edges // 2
    return pl.pallas_call(
        prep_body,
        out_shape=[
            pltpu.HBM((total, padded), bf16),
            pltpu.HBM((live, total), bf16),
            pltpu.HBM((batches, 8, edges), f32),
            pltpu.HBM((batches, edges, LANES), f32),
        ],
        compiler_params=room(24),
        name="prep",
    )(slots, negs)


def lanes_of(shape):
    return lax.broadcasted_iota(jnp.int32, shape, 1)


def leftover(blocks):
    lane = lanes_of(blocks[0].shape)
    out = blocks[-1]
    for block in blocks[-2::-1]:
        out = pltpu.roll(jnp.where(lane < MAIN, out, block), SPARE, 1)
    return out


def grads_body(heads, tails, by_edge, by_slot, count_row, count_col, ahead, out_heads, out_tails,
               high, low, extra, d_high, d_low, edge_part, slot_part, summed, packed, in_sems, out_sems):
    live = by_slot.shape[0]
    head_count = live - tails.shape[0]
    owners = head_count // 8
    tall = heads.shape[0] // owners
    padded = by_edge.shape[1]
    width = tails.shape[1]
    batches, _, edges = count_row.shape
    loads = []
    for p in range(2 * batches):
        span = pl.ds(p * edges, edges)
        loads.append(pltpu.make_async_copy(by_edge.at[span], edge_part.at[span], in_sems.at[p]))
        loads[-1].start()
    last = pltpu.make_async_copy(by_slot, slot_part, in_sems.at[2 * batches])
    last.start()
    ends = heads[pl.ds(tall - 1, owners, stride=tall), :]
    for k in range(8):
        span = slice(k * owners, (k + 1) * owners)
        for c in range(QUARTERS):
            lanes = slice(c * LANES, (c + 1) * LANES)
            if c < QUARTERS - 1:
                block = heads[pl.ds(8 * c + k, owners, stride=tall), :]
            else:
                block = pltpu.roll(ends, (LANES - 16 * k) % LANES, 1) if k else ends
                block = jnp.where(lanes_of(block.shape) < 16, block, 0.0)
            high[span, lanes], low[span, lanes] = halves(block)
    pieces = list(halves(tails[...]))
    pieces.append(jnp.zeros((padded - head_count - 2 * tails.shape[0], width), bf16))
    extra[...] = jnp.concatenate(pieces, axis=0)

    def gathered(b):
        picks = []
        for side in range(2):
            at = (2 * b + side) * edges
            loads[2 * b + side].wait()
            chosen = edge_part[at : at + edges, :head_count]
            rest = edge_part[at : at + edges, head_count:]
            picks.append(mm(chosen, high[...]) + mm(chosen, low[...]) + mm(rest, extra[...]))
        return picks

    def gained(b, scores):
        decay = jnp.exp2(jnp.minimum(scores * -LOG2E, 126.0))
        weight = 1.0 / (1.0 + decay)
        counts = count_row[b, 0:1, :] + jnp.concatenate([count_col[b]] * (edges // LANES), axis=1)
        return halves(weight * counts)

    def pulled(at, gain, rest, pull, rows_high, rows_low, rows):
        moved = mm(gain, rows_high) + mm(gain, rows_low) + mm(rest, rows_high) + pull * rows
        d_high[at : at + edges, :], d_low[at : at + edges, :] = halves(moved)

    for b in range(batches):
        s_rows, t_rows = gathered(b)
        s_high, s_low = halves(s_rows)
        t_high, t_low = halves(t_rows)
        positive = jnp.sum(s_rows * t_rows, axis=1, keepdims=True)
        falling = jnp.exp(-jnp.abs(positive))
        pull = -jnp.where(positive >= 0, falling, 1.0) / (1.0 + falling)
        gain, rest = gained(b, mm_nt(s_high, t_high) + mm_nt(s_high, t_low) + mm_nt(s_low, t_high))
        pulled(2 * b * edges, gain, rest, pull, t_high, t_low, t_rows)
        pulled((2 * b + 1) * edges, gain.T, rest.T, pull, s_high, s_low, s_rows)
    last.wait()
    stores = []
    block = 2 * LANES
    short = 7 * owners
    for h in range(width // block):
        span = slice(h * block, (h + 1) * block)
        summed[:, span] = mm(slot_part[...], d_high[:, span]) + mm(slot_part[...], d_low[:, span])
        for q in (2 * h, 2 * h + 1):

            def quarter(at, size):
                if q < QUARTERS - 1:
                    return summed[at : at + size, q * LANES : (q + 1) * LANES]
                return leftover([summed[at : at + size, c * LANES : (c + 1) * LANES] for c in range(QUARTERS)])

            eighth = quarter(7 * owners, owners)
            for k in range(7):
                value = quarter(k * owners, owners)
                if SPARE * k < MAIN:
                    moved = pltpu.roll(eighth, (MAIN - SPARE * k) % LANES, 1)
                    value = jnp.where(lanes_of(value.shape) < MAIN, value, moved)
                packed[pl.ds(q * short + k, owners, stride=7), :] = value
            out_tails[:, q * LANES : (q + 1) * LANES] = quarter(head_count, live - head_count)
        part = pl.ds(2 * h * short, 2 * short)
        stores.append(pltpu.make_async_copy(packed.at[part], out_heads.at[part], out_sems.at[h]))
        stores[-1].start()
    for store in stores:
        store.wait()


def grads(heads, tails, by_edge, by_slot, count_row, count_col, ahead):
    width = tails.shape[1]
    total, padded = by_edge.shape
    live = by_slot.shape[0]
    shape = (QUARTERS * 7 * (live - tails.shape[0]) // 8, LANES)
    return pl.pallas_call(
        grads_body,
        in_specs=[VMEM, VMEM, HBM, HBM, VMEM, VMEM, HBM],
        out_specs=[HBM, VMEM],
        out_shape=[pltpu.HBM(shape, f32), jax.ShapeDtypeStruct(tails.shape, f32)],
        scratch_shapes=[
            pltpu.VMEM((live - tails.shape[0], width), bf16),
            pltpu.VMEM((live - tails.shape[0], width), bf16),
            pltpu.VMEM((padded - live + tails.shape[0], width), bf16),
            pltpu.VMEM((total, width), bf16),
            pltpu.VMEM((total, width), bf16),
            pltpu.VMEM(by_edge.shape, bf16),
            pltpu.VMEM(by_slot.shape, bf16),
            pltpu.VMEM((live, width), f32),
            pltpu.VMEM(shape, f32),
            pltpu.SemaphoreType.DMA((2 * count_row.shape[0] + 1,)),
            pltpu.SemaphoreType.DMA((width // LANES // 2,)),
        ],
        compiler_params=room(48),
        name="grads",
    )(near(heads), tails, far(by_edge), far(by_slot), count_row, count_col, far(ahead))


def hot_body(me, *refs):
    lists, hot = refs[:-1], refs[-1]
    rows = hot.shape[0]
    groups = len(lists)
    tail_count = HEAVY * 8
    head_count = lists[0].shape[1] - tail_count
    for s, ids in enumerate(lists):
        group = (me[0] + s) % groups
        down = lax.broadcasted_iota(jnp.int32, (rows, head_count), 0)
        spot = pl.multiple_of(group * head_count, LANES)
        hot[:, pl.ds(spot, head_count)] = jnp.where(down == ids[:, :head_count], 1.0, 0.0).astype(bf16)
    tails = jnp.concatenate([ids[:, head_count:] for ids in lists], axis=1)
    down = lax.broadcasted_iota(jnp.int32, (rows, tails.shape[1]), 0)
    hot[:, groups * head_count :] = jnp.where(down == tails, 1.0, 0.0).astype(bf16)


def hot_rows(me, lists, rows):
    vmem = pl.BlockSpec(memory_space=pltpu.VMEM)
    return pl.pallas_call(
        hot_body,
        in_specs=[pl.BlockSpec(memory_space=pltpu.SMEM)] + [vmem] * len(lists),
        out_shape=pltpu.HBM((rows, len(lists) * lists[0].shape[1]), bf16),
        compiler_params=room(16),
        name="hot",
    )(me, *lists)


def owner_body(back, tails, hot, out, spots, sems):
    parts = sems.shape[0] - 1
    short = back.shape[0] // parts
    each = short // 7 * 8
    owners = short // 7
    spans = [(p * each, each) for p in range(parts)] + [(parts * each, tails.shape[0])]
    loads = []
    for p, (at, size) in enumerate(spans):
        loads.append(pltpu.make_async_copy(hot.at[:, pl.ds(at, size)], spots.at[:, pl.ds(at, size)], sems.at[p]))
        loads[-1].start()
    total = None
    for p, (at, size) in enumerate(spans):
        if p < parts:
            eighth = jnp.zeros((owners, LANES), f32)
            lane = lanes_of(eighth.shape)
            for k in range(-(-MAIN // SPARE)):
                moved = pltpu.roll(back[pl.ds(p * short + k, owners, stride=7), :], (SPARE * k - MAIN) % LANES, 1)
                eighth = jnp.where((lane >= SPARE * k) & (lane < SPARE * (k + 1)), moved, eighth)
            values = jnp.concatenate([back[p * short : (p + 1) * short, :], eighth], axis=0)
        else:
            values = tails[...]
        both = jnp.concatenate(halves(values), axis=1)
        loads[p].wait()
        part = mm(spots[:, at : at + size], both)
        total = part if total is None else total + part
    summed = total[:, :LANES] + total[:, LANES:]
    out[...] = summed.T[: out.shape[0], :]


def owner(back, tails, hot):
    return pl.pallas_call(
        owner_body,
        in_specs=[VMEM, VMEM, HBM],
        out_specs=VMEM,
        out_shape=jax.ShapeDtypeStruct((MAIN, hot.shape[0]), f32),
        scratch_shapes=[pltpu.VMEM(hot.shape, bf16), pltpu.SemaphoreType.DMA((5,))],
        compiler_params=room(16),
        name="owner",
    )(near(back), tails, far(hot))


def update_body(me, own, next1, next2, next3, rows, sums, new_rows, new_sums, quarters, fresh_rows, sems):
    for s, piece in enumerate((own, next1, next2, next3)):
        quarters[(me[0] + 4 - s) % 4] = piece[...]
    squares = jnp.zeros(sums.shape, f32)
    for q in range(QUARTERS):
        squares += jnp.sum(quarters[q] * quarters[q], axis=0, keepdims=True)
    fresh = sums[...] + squares * (1.0 / rows.shape[0])
    new_sums[...] = fresh
    scale = LEARN_RATE / jnp.sqrt(fresh)
    depth = rows.shape[0]
    stores = []
    for c in range(QUARTERS - 1):
        at = c * LANES
        end = at + LANES
        wide = SPARE
        if c == QUARTERS - 2:
            end = depth
            wide = depth - at - MAIN
        main = slice(at, at + MAIN)
        rest = slice(at + MAIN, end)
        fresh_rows[main, :] = rows[main, :] - quarters[c] * scale
        fresh_rows[rest, :] = rows[rest, :] - quarters[QUARTERS - 1, SPARE * c : SPARE * c + wide, :] * scale
        span = pl.ds(at, end - at)
        stores.append(pltpu.make_async_copy(fresh_rows.at[span], new_rows.at[span], sems.at[c]))
        stores[-1].start()
    for store in stores:
        store.wait()


def update(me, pieces, rows, sums):
    return pl.pallas_call(
        update_body,
        in_specs=[SMEM] + [VMEM] * len(pieces) + [VMEM, VMEM],
        out_specs=[HBM, VMEM],
        out_shape=[
            jax.ShapeDtypeStruct(rows.shape, f32),
            jax.ShapeDtypeStruct(sums.shape, f32),
        ],
        scratch_shapes=[
            pltpu.VMEM((len(pieces), *pieces[0].shape), f32),
            pltpu.VMEM(rows.shape, f32),
            pltpu.SemaphoreType.DMA((len(pieces),)),
        ],
        compiler_params=room(16),
        name="update",
    )(me, *[near(piece) for piece in pieces], near(rows), sums)


def compact(slots, here, owners, capacity):
    half = capacity // 2
    who, k = slots // capacity, slots % capacity
    return jnp.where(k < half, k * owners + who, owners * half + (who - here) % owners * half + k - half)


def local(embedding, adagrad_sum, row_lists, source_slots, target_slots, negative_ids):
    requests = row_lists[0, 0]
    owners, capacity = requests.shape
    half = capacity // 2
    rows = embedding.shape[0]
    groups = lax.axis_size("rep")
    edges = source_slots.shape[3]
    here = lax.axis_index("dom")
    given = exchanged(requests.reshape(owners, 1, capacity), "dom")
    incoming = given.reshape(owners, capacity)
    columns = embedding.T
    spread = spread_rows(columns)
    slots = jnp.stack([source_slots[0, 0], target_slots[0, 0]], axis=1).reshape(1, -1)
    slots = compact(slots, here, owners, capacity)
    live = owners * half + HEAVY * half
    padded = -(-live // LANES) * LANES
    plan = prep(slots, negative_ids[0, 0].reshape(1, -1), edges, live, padded)

    heads, tails = serve(given, here.reshape(1).astype(jnp.int32), spread)
    tails = tails.reshape(HEAVY, half, -1)
    tails = jnp.concatenate(
        [tails[0]] + [passed_along(tails[r], "dom", -r) for r in range(1, HEAVY)], axis=0
    )
    heads = exchanged(heads.reshape(owners, -1, 1, LANES), "dom").reshape(-1, LANES)
    me = lax.axis_index("rep")
    mine = me.reshape(1).astype(jnp.int32)
    askers = jnp.arange(owners)[None, :] == ((here - jnp.arange(HEAVY)) % owners)[:, None]
    tail_ids = jnp.sum(jnp.where(askers[:, :, None], incoming[None, :, half:], 0), axis=1)
    ids = [incoming[:, : half - 1], incoming[:, half - 1], tail_ids]
    ids = jnp.concatenate([part.reshape(1, -1) for part in ids], axis=1)
    listed = [ids] + [passed_along(ids, "rep", -s) for s in range(1, groups)]
    hot = hot_rows(mine, listed, rows)

    head_grads, tail_grads = grads(heads, tails, *plan, hot)
    back = exchanged(head_grads.reshape(groups * owners, half - 1, 1, LANES), ("rep", "dom"))
    tail_grads = jnp.moveaxis(tail_grads.reshape(HEAVY * half, groups, LANES), 1, 0)
    wanted = [
        lax.dynamic_index_in_dim(tail_grads, (me + groups - s) % groups, 0, keepdims=False)
        for s in range(groups)
    ]
    tail_grads = jnp.stack(
        [wanted[0]] + [passed_along(wanted[s], "rep", -s) for s in range(1, groups)], axis=0
    ).reshape(groups, HEAVY, half, LANES)
    tail_back = [tail_grads[:, 0]] + [passed_along(tail_grads[:, r], "dom", r) for r in range(1, HEAVY)]
    tail_back = jnp.stack(tail_back, axis=1).reshape(-1, LANES)
    quarter = owner(back.reshape(-1, LANES), tail_back, hot)
    pieces = [quarter] + [passed_along(quarter, "rep", s) for s in range(1, groups)]
    new_rows, new_sums = update(mine, pieces, columns, adagrad_sum.reshape(1, -1))
    return new_rows.T, new_sums.reshape(-1)


def solution(mesh):
    in_specs = (
        P("dom", None),
        P("dom"),
        P("rep", "dom", None, None),
        P("rep", "dom", None, None),
        P("rep", "dom", None, None),
        P("rep", "dom", None, None, None),
    )
    out_specs = (P("dom", None), P("dom"))

    return jax.shard_map(local, mesh=mesh, in_specs=in_specs, out_specs=out_specs, check_vma=False)
```

```python
import jax
import jax.numpy as jnp
from jax import lax
from jax.experimental import pallas as pl
from jax.experimental.pallas import tpu as pltpu
from jax.sharding import PartitionSpec as P


HEAVY = 4
LEARN_RATE = 0.1
LOG2E = 1.4426950408889634
LANES = 128
MAIN = 104
SPARE = LANES - MAIN
QUARTERS = 4
CUT = 56
f32 = jnp.float32
bf16 = jnp.bfloat16


def passed_along(value, axis, steps):
    count = lax.axis_size(axis)
    pairs = [(source, (source + steps) % count) for source in range(count)]
    return lax.ppermute(value, axis, pairs)


def exchanged(value, axis):
    return lax.all_to_all(value, axis, 0, 0, tiled=True)


def halves(x):
    high = x.astype(bf16)
    low = (x - high.astype(f32)).astype(bf16)
    return high, low


VMEM = pl.BlockSpec(memory_space=pltpu.VMEM)
SMEM = pl.BlockSpec(memory_space=pltpu.SMEM)
HBM = pl.BlockSpec(memory_space=pltpu.HBM)


def room(mib):
    return pltpu.CompilerParams(vmem_limit_bytes=mib << 20)


def far(x):
    return pltpu.with_memory_space_constraint(x, pltpu.HBM)


def near(x):
    return pltpu.with_memory_space_constraint(x, pltpu.VMEM)


def mm(a, b):
    return jnp.dot(a, b, preferred_element_type=f32)


def mm_nt(a, b):
    return lax.dot_general(a, b, (((1,), (1,)), ((), ())), preferred_element_type=f32)


def spread_body(columns, out):
    depth, rows = columns.shape
    for c in range(out.shape[1]):
        piece = columns[c * LANES : min((c + 1) * LANES, depth), :]
        if piece.shape[0] < LANES:
            piece = jnp.concatenate([piece, jnp.zeros((LANES - piece.shape[0], rows), f32)], axis=0)
        out[:, c, :] = piece.T


def spread_rows(columns):
    return pl.pallas_call(
        spread_body,
        out_specs=VMEM,
        out_shape=pltpu.VMEM((columns.shape[1], QUARTERS, LANES), f32),
        compiler_params=room(16),
        name="spread",
    )(columns)


def serve_body(ids, here, rows, heads, tails, picked, ends, sems):
    owners = ids.shape[0]
    parts = sems.shape[0]
    each = owners // parts
    blocks = QUARTERS - 1
    tall = 8 * blocks + 1

    def eight(w, carry):
        taken = [rows[ids[w, 0, k]] for k in range(8)]
        for k in range(8):
            picked[pl.ds(w * tall + k, blocks, stride=8), :] = taken[k][:blocks]
            ends[pl.ds(w * 8 + k, 1), :] = taken[k][blocks:]
        return carry

    for reach in range(HEAVY):
        asker = (here[0] + owners - reach) % owners
        for k in range(8):
            row = rows[ids[asker, 0, 8 + k]]
            for c in range(QUARTERS):
                tails[reach * 8 + k : reach * 8 + k + 1, c * LANES : (c + 1) * LANES] = row[c : c + 1]
    copies = []
    for part in range(parts):
        lax.fori_loop(part * each, (part + 1) * each, eight, 0, unroll=4)
        joined = ends[pl.ds(part * each * 8, each, stride=8), :]
        for k in range(1, 8):
            joined += pltpu.roll(ends[pl.ds(part * each * 8 + k, each, stride=8), :], 16 * k, 1)
        picked[pl.ds(part * each * tall + tall - 1, each, stride=tall), :] = joined
        span = pl.ds(part * each * tall, each * tall)
        copies.append(pltpu.make_async_copy(picked.at[span], heads.at[span], sems.at[part]))
        copies[-1].start()
    for copy in copies:
        copy.wait()


def serve(ids, here, rows):
    width = QUARTERS * LANES
    owners = ids.shape[0]
    shape = (owners * (8 * (QUARTERS - 1) + 1), LANES)
    return pl.pallas_call(
        serve_body,
        in_specs=[SMEM, SMEM, VMEM],
        out_specs=[HBM, VMEM],
        out_shape=[pltpu.HBM(shape, f32), jax.ShapeDtypeStruct((HEAVY * 8, width), f32)],
        scratch_shapes=[
            pltpu.VMEM(shape, f32),
            pltpu.VMEM((owners * 8, LANES), f32),
            pltpu.SemaphoreType.DMA((4,)),
        ],
        compiler_params=room(16),
        name="serve",
    )(ids, here, near(rows))


def prep_body(slots, negs, by_edge, by_slot, count_row, count_col):
    edges = count_row.shape[2]
    parts = slots.shape[1] // edges
    live = by_slot.shape[0]
    padded = by_edge.shape[1]
    one, zero = jnp.ones((), f32), jnp.zeros((), f32)
    for p in range(parts):
        row = slots[:, p * edges : (p + 1) * edges]
        down = lax.broadcasted_iota(jnp.int32, (live, edges), 0)
        by_slot[:, p * edges : (p + 1) * edges] = jnp.where(down == row, one, zero).astype(bf16)
        column = jnp.broadcast_to(row, (LANES, edges)).T
        across = lax.broadcasted_iota(jnp.int32, (edges, LANES), 1)
        blocks = padded // LANES
        for c in range(blocks):
            hit = across + c * LANES == column
            if c == blocks - 1:
                count = HEAVY * 8
                hit = hit | ((across >= count) & (across + (c * LANES - count) == column))
            by_edge[p * edges : (p + 1) * edges, c * LANES : (c + 1) * LANES] = jnp.where(hit, one, zero).astype(bf16)
        neg = negs[:, p * edges : (p + 1) * edges]
        down = lax.broadcasted_iota(jnp.int32, (edges, edges), 0)
        drawn = jnp.where(down == neg, one, zero).astype(bf16)
        if p % 2 == 0:
            count_row[p // 2] = mm_nt(jnp.ones((8, edges), bf16), drawn) * (1.0 / edges)
        else:
            count_col[p // 2] = mm(drawn, jnp.ones((edges, LANES), bf16)) * (1.0 / edges)


def prep(slots, negs, edges, live, padded):
    total = slots.shape[1]
    batches = total // edges // 2
    return pl.pallas_call(
        prep_body,
        out_shape=[
            pltpu.HBM((total, padded), bf16),
            pltpu.HBM((live, total), bf16),
            pltpu.HBM((batches, 8, edges), f32),
            pltpu.HBM((batches, edges, LANES), f32),
        ],
        compiler_params=room(24),
        name="prep",
    )(slots, negs)


def lanes_of(shape):
    return lax.broadcasted_iota(jnp.int32, shape, 1)


def leftover(blocks):
    lane = lanes_of(blocks[0].shape)
    out = blocks[-1]
    for block in blocks[-2::-1]:
        out = pltpu.roll(jnp.where(lane < MAIN, out, block), SPARE, 1)
    return out


def grads_body(heads, tails, by_edge, by_slot, count_row, count_col, ahead, out_heads, out_tails,
               high, low, extra, d_high, d_low, edge_part, slot_part, summed, packed, in_sems, out_sems):
    live = by_slot.shape[0]
    head_count = live - tails.shape[0]
    owners = head_count // 8
    tall = heads.shape[0] // owners
    padded = by_edge.shape[1]
    width = tails.shape[1]
    batches, _, edges = count_row.shape
    loads = []
    for p in range(2 * batches):
        span = pl.ds(p * edges, edges)
        loads.append(pltpu.make_async_copy(by_edge.at[span], edge_part.at[span], in_sems.at[p]))
        loads[-1].start()
    last = pltpu.make_async_copy(by_slot, slot_part, in_sems.at[2 * batches])
    last.start()
    ends = heads[pl.ds(tall - 1, owners, stride=tall), :]
    for k in range(8):
        span = slice(k * owners, (k + 1) * owners)
        for c in range(QUARTERS):
            lanes = slice(c * LANES, (c + 1) * LANES)
            if c < QUARTERS - 1:
                block = heads[pl.ds(8 * c + k, owners, stride=tall), :]
            else:
                block = pltpu.roll(ends, (LANES - 16 * k) % LANES, 1) if k else ends
                block = jnp.where(lanes_of(block.shape) < 16, block, 0.0)
            high[span, lanes], low[span, lanes] = halves(block)
    pieces = list(halves(tails[...]))
    pieces.append(jnp.zeros((padded - head_count - 2 * tails.shape[0], width), bf16))
    extra[...] = jnp.concatenate(pieces, axis=0)

    def gathered(b):
        picks = []
        for side in range(2):
            at = (2 * b + side) * edges
            loads[2 * b + side].wait()
            chosen = edge_part[at : at + edges, :head_count]
            rest = edge_part[at : at + edges, head_count:]
            picks.append(mm(chosen, high[...]) + mm(chosen, low[...]) + mm(rest, extra[...]))
        return picks

    def gained(b, scores):
        decay = jnp.exp2(jnp.minimum(scores * -LOG2E, 126.0))
        weight = 1.0 / (1.0 + decay)
        counts = count_row[b, 0:1, :] + jnp.concatenate([count_col[b]] * (edges // LANES), axis=1)
        return halves(weight * counts)

    def pulled(at, gain, rest, pull, rows_high, rows_low, rows):
        moved = mm(gain, rows_high) + mm(gain, rows_low) + mm(rest, rows_high) + pull * rows
        d_high[at : at + edges, :], d_low[at : at + edges, :] = halves(moved)

    for b in range(batches):
        s_rows, t_rows = gathered(b)
        s_high, s_low = halves(s_rows)
        t_high, t_low = halves(t_rows)
        positive = jnp.sum(s_rows * t_rows, axis=1, keepdims=True)
        falling = jnp.exp(-jnp.abs(positive))
        pull = -jnp.where(positive >= 0, falling, 1.0) / (1.0 + falling)
        gain, rest = gained(b, mm_nt(s_high, t_high) + mm_nt(s_high, t_low) + mm_nt(s_low, t_high))
        pulled(2 * b * edges, gain, rest, pull, t_high, t_low, t_rows)
        pulled((2 * b + 1) * edges, gain.T, rest.T, pull, s_high, s_low, s_rows)
    last.wait()
    stores = []
    block = 2 * LANES
    short = 7 * owners
    for h in range(width // block):
        span = slice(h * block, (h + 1) * block)
        summed[:, span] = mm(slot_part[...], d_high[:, span]) + mm(slot_part[...], d_low[:, span])
        for q in (2 * h, 2 * h + 1):

            def quarter(at, size):
                if q < QUARTERS - 1:
                    return summed[at : at + size, q * LANES : (q + 1) * LANES]
                return leftover([summed[at : at + size, c * LANES : (c + 1) * LANES] for c in range(QUARTERS)])

            eighth = quarter(7 * owners, owners)
            for k in range(7):
                value = quarter(k * owners, owners)
                if SPARE * k < MAIN:
                    moved = pltpu.roll(eighth, (MAIN - SPARE * k) % LANES, 1)
                    value = jnp.where(lanes_of(value.shape) < MAIN, value, moved)
                packed[pl.ds(q * short + k, owners, stride=7), :] = value
            out_tails[:, q * LANES : (q + 1) * LANES] = quarter(head_count, live - head_count)
        part = pl.ds(2 * h * short, 2 * short)
        stores.append(pltpu.make_async_copy(packed.at[part], out_heads.at[part], out_sems.at[h]))
        stores[-1].start()
    for store in stores:
        store.wait()


def grads(heads, tails, by_edge, by_slot, count_row, count_col, ahead):
    width = tails.shape[1]
    total, padded = by_edge.shape
    live = by_slot.shape[0]
    shape = (QUARTERS * 7 * (live - tails.shape[0]) // 8, LANES)
    return pl.pallas_call(
        grads_body,
        in_specs=[VMEM, VMEM, HBM, HBM, VMEM, VMEM, HBM],
        out_specs=[HBM, VMEM],
        out_shape=[pltpu.HBM(shape, f32), jax.ShapeDtypeStruct(tails.shape, f32)],
        scratch_shapes=[
            pltpu.VMEM((live - tails.shape[0], width), bf16),
            pltpu.VMEM((live - tails.shape[0], width), bf16),
            pltpu.VMEM((padded - live + tails.shape[0], width), bf16),
            pltpu.VMEM((total, width), bf16),
            pltpu.VMEM((total, width), bf16),
            pltpu.VMEM(by_edge.shape, bf16),
            pltpu.VMEM(by_slot.shape, bf16),
            pltpu.VMEM((live, width), f32),
            pltpu.VMEM(shape, f32),
            pltpu.SemaphoreType.DMA((2 * count_row.shape[0] + 1,)),
            pltpu.SemaphoreType.DMA((width // LANES // 2,)),
        ],
        compiler_params=room(48),
        name="grads",
    )(near(heads), tails, far(by_edge), far(by_slot), count_row, count_col, far(ahead))


def hot_body(me, *refs):
    lists, hot = refs[:-1], refs[-1]
    rows = hot.shape[0]
    groups = len(lists)
    tail_count = HEAVY * 8
    head_count = lists[0].shape[1] - tail_count
    for s, ids in enumerate(lists):
        group = (me[0] + s) % groups
        down = lax.broadcasted_iota(jnp.int32, (rows, head_count), 0)
        spot = pl.multiple_of(group * head_count, LANES)
        hot[:, pl.ds(spot, head_count)] = jnp.where(down == ids[:, :head_count], 1.0, 0.0).astype(bf16)
    tails = jnp.concatenate([ids[:, head_count:] for ids in lists], axis=1)
    down = lax.broadcasted_iota(jnp.int32, (rows, tails.shape[1]), 0)
    hot[:, groups * head_count :] = jnp.where(down == tails, 1.0, 0.0).astype(bf16)


def hot_rows(me, lists, rows):
    vmem = pl.BlockSpec(memory_space=pltpu.VMEM)
    return pl.pallas_call(
        hot_body,
        in_specs=[pl.BlockSpec(memory_space=pltpu.SMEM)] + [vmem] * len(lists),
        out_shape=pltpu.HBM((rows, len(lists) * lists[0].shape[1]), bf16),
        compiler_params=room(16),
        name="hot",
    )(me, *lists)


def owner_body(back, tails, hot, first, second, spots, sems):
    parts = sems.shape[0] - 1
    short = back.shape[0] // parts
    each = short // 7 * 8
    owners = short // 7
    spans = [(p * each, each) for p in range(parts)] + [(parts * each, tails.shape[0])]
    loads = []
    for p, (at, size) in enumerate(spans):
        loads.append(pltpu.make_async_copy(hot.at[:, pl.ds(at, size)], spots.at[:, pl.ds(at, size)], sems.at[p]))
        loads[-1].start()
    total = None
    for p, (at, size) in enumerate(spans):
        if p < parts:
            eighth = jnp.zeros((owners, LANES), f32)
            lane = lanes_of(eighth.shape)
            for k in range(-(-MAIN // SPARE)):
                moved = pltpu.roll(back[pl.ds(p * short + k, owners, stride=7), :], (SPARE * k - MAIN) % LANES, 1)
                eighth = jnp.where((lane >= SPARE * k) & (lane < SPARE * (k + 1)), moved, eighth)
            values = jnp.concatenate([back[p * short : (p + 1) * short, :], eighth], axis=0)
        else:
            values = tails[...]
        both = jnp.concatenate(halves(values), axis=1)
        loads[p].wait()
        part = mm(spots[:, at : at + size], both)
        total = part if total is None else total + part
    summed = total[:, :LANES] + total[:, LANES:]
    turned = summed.T
    first[...] = turned[:CUT, :]
    second[...] = turned[CUT:MAIN, :]


def owner(back, tails, hot):
    return pl.pallas_call(
        owner_body,
        in_specs=[VMEM, VMEM, HBM],
        out_specs=[VMEM, VMEM],
        out_shape=[
            jax.ShapeDtypeStruct((CUT, hot.shape[0]), f32),
            jax.ShapeDtypeStruct((MAIN - CUT, hot.shape[0]), f32),
        ],
        scratch_shapes=[pltpu.VMEM(hot.shape, bf16), pltpu.SemaphoreType.DMA((5,))],
        compiler_params=room(16),
        name="owner",
    )(near(back), tails, far(hot))


def update_body(me, *refs):
    pieces, (rows, sums, new_rows, new_sums, quarters, fresh_rows, sems) = refs[:-7], refs[-7:]
    for s in range(QUARTERS):
        spot = (me[0] + QUARTERS - s) % QUARTERS
        quarters[spot, :CUT, :] = pieces[2 * s][...]
        quarters[spot, CUT:, :] = pieces[2 * s + 1][...]
    squares = jnp.zeros(sums.shape, f32)
    for q in range(QUARTERS):
        squares += jnp.sum(quarters[q] * quarters[q], axis=0, keepdims=True)
    fresh = sums[...] + squares * (1.0 / rows.shape[0])
    new_sums[...] = fresh
    scale = LEARN_RATE / jnp.sqrt(fresh)
    depth = rows.shape[0]
    stores = []
    for c in range(QUARTERS - 1):
        at = c * LANES
        end = at + LANES
        wide = SPARE
        if c == QUARTERS - 2:
            end = depth
            wide = depth - at - MAIN
        main = slice(at, at + MAIN)
        rest = slice(at + MAIN, end)
        fresh_rows[main, :] = rows[main, :] - quarters[c] * scale
        fresh_rows[rest, :] = rows[rest, :] - quarters[QUARTERS - 1, SPARE * c : SPARE * c + wide, :] * scale
        span = pl.ds(at, end - at)
        stores.append(pltpu.make_async_copy(fresh_rows.at[span], new_rows.at[span], sems.at[c]))
        stores[-1].start()
    for store in stores:
        store.wait()


def update(me, pieces, rows, sums):
    return pl.pallas_call(
        update_body,
        in_specs=[SMEM] + [VMEM] * len(pieces) + [VMEM, VMEM],
        out_specs=[HBM, VMEM],
        out_shape=[
            jax.ShapeDtypeStruct(rows.shape, f32),
            jax.ShapeDtypeStruct(sums.shape, f32),
        ],
        scratch_shapes=[
            pltpu.VMEM((QUARTERS, MAIN, rows.shape[1]), f32),
            pltpu.VMEM(rows.shape, f32),
            pltpu.SemaphoreType.DMA((QUARTERS,)),
        ],
        compiler_params=room(16),
        name="update",
    )(me, *[near(piece) for piece in pieces], near(rows), sums)


def compact(slots, here, owners, capacity):
    half = capacity // 2
    who, k = slots // capacity, slots % capacity
    return jnp.where(k < half, k * owners + who, owners * half + (who - here) % owners * half + k - half)


def local(embedding, adagrad_sum, row_lists, source_slots, target_slots, negative_ids):
    requests = row_lists[0, 0]
    owners, capacity = requests.shape
    half = capacity // 2
    rows = embedding.shape[0]
    groups = lax.axis_size("rep")
    edges = source_slots.shape[3]
    here = lax.axis_index("dom")
    given = exchanged(requests.reshape(owners, 1, capacity), "dom")
    incoming = given.reshape(owners, capacity)
    columns = embedding.T
    spread = spread_rows(columns)
    slots = jnp.stack([source_slots[0, 0], target_slots[0, 0]], axis=1).reshape(1, -1)
    slots = compact(slots, here, owners, capacity)
    live = owners * half + HEAVY * half
    padded = -(-live // LANES) * LANES
    plan = prep(slots, negative_ids[0, 0].reshape(1, -1), edges, live, padded)

    heads, tails = serve(given, here.reshape(1).astype(jnp.int32), spread)
    tails = tails.reshape(HEAVY, half, -1)
    tails = jnp.concatenate(
        [tails[0]] + [passed_along(tails[r], "dom", -r) for r in range(1, HEAVY)], axis=0
    )
    heads = exchanged(heads.reshape(owners, -1, 1, LANES), "dom").reshape(-1, LANES)
    me = lax.axis_index("rep")
    mine = me.reshape(1).astype(jnp.int32)
    askers = jnp.arange(owners)[None, :] == ((here - jnp.arange(HEAVY)) % owners)[:, None]
    tail_ids = jnp.sum(jnp.where(askers[:, :, None], incoming[None, :, half:], 0), axis=1)
    ids = [incoming[:, : half - 1], incoming[:, half - 1], tail_ids]
    ids = jnp.concatenate([part.reshape(1, -1) for part in ids], axis=1)
    listed = [ids] + [passed_along(ids, "rep", -s) for s in range(1, groups)]
    hot = hot_rows(mine, listed, rows)

    head_grads, tail_grads = grads(heads, tails, *plan, hot)
    back = exchanged(head_grads.reshape(groups * owners, half - 1, 1, LANES), ("rep", "dom"))
    tail_grads = jnp.moveaxis(tail_grads.reshape(HEAVY * half, groups, LANES), 1, 0)
    wanted = [
        lax.dynamic_index_in_dim(tail_grads, (me + groups - s) % groups, 0, keepdims=False)
        for s in range(groups)
    ]
    tail_grads = jnp.stack(
        [wanted[0]] + [passed_along(wanted[s], "rep", -s) for s in range(1, groups)], axis=0
    ).reshape(groups, HEAVY, half, LANES)
    tail_back = [tail_grads[:, 0]] + [passed_along(tail_grads[:, r], "dom", r) for r in range(1, HEAVY)]
    tail_back = jnp.stack(tail_back, axis=1).reshape(-1, LANES)
    first, second = owner(back.reshape(-1, LANES), tail_back, hot)
    down_second = passed_along(second, "rep", -1)
    down_first = passed_along(first, "rep", -1)
    up_first = passed_along(first, "rep", 1)
    over_first = passed_along(first, "rep", 2)
    up_second = passed_along(second, "rep", 1)
    over_second = passed_along(down_second, "rep", -1)
    pieces = [first, second, up_first, up_second, over_first, over_second, down_first, down_second]
    new_rows, new_sums = update(mine, pieces, columns, adagrad_sum.reshape(1, -1))
    return new_rows.T, new_sums.reshape(-1)


def solution(mesh):
    in_specs = (
        P("dom", None),
        P("dom"),
        P("rep", "dom", None, None),
        P("rep", "dom", None, None),
        P("rep", "dom", None, None),
        P("rep", "dom", None, None, None),
    )
    out_specs = (P("dom", None), P("dom"))

    return jax.shard_map(local, mesh=mesh, in_specs=in_specs, out_specs=out_specs, check_vma=False)
```
